32 devices in a mesh: groups: 2 (over x), wide: 16 (over z, y, core).
Axes of the slice: x: 2, y: 2, z: 4, core: 2. Of those that a mesh axis runs over, the one named last changes fastest.
Arguments:
- frames: bfloat16 [2048, 3072], P(('groups', 'wide')), parts along dimension 0, may hold values from -6 to 6
- latent_len: int32 [64], P('groups'), parts along dimension 0, may hold values from 1 to 9, as said below
- reader: int32 [64], P('groups'), parts along dimension 0, may hold values from 0 to 15, as said below
- owner: int32 [64], P('groups'), parts along dimension 0, may hold values from 0 to 15, as said below
- w_in: bfloat16 [128, 81], replicated, may hold values from -0.625 to 0.625
- b_in: float32 [128], replicated, may hold values from -3 to 3
- g_in: float32 [128], replicated, may hold values from 0.25 to 1.75
- w_down: bfloat16 [128, 512], replicated, may hold values from -0.25 to 0.25
- b_down: float32 [128], replicated, may hold values from -3 to 3
- g_down: float32 [128], replicated, may hold values from 0.25 to 1.75
- w_head: bfloat16 [16, 8192], replicated, may hold values from -0.0625 to 0.0625
- b_head: float32 [16], replicated, may hold values from -3 to 3
Outputs:
- latents: bfloat16 [576, 256], P(('groups', 'wide')), parts along dimension 0
The draws below stay inside these ranges and needn't reach their ends.
There are 2 independent parts, one for each index of `groups`. The reference program is written for one: setup_inputs(seed, part) draws one part's arguments, and reference() takes and returns one part's arrays. A program takes and returns all parts, laid end to end along the dimension named above; an argument that names none is the same for every part. Nothing has to cross between parts.
Inputs may be any that keep to these rules, and one draw needn't show every extreme that they name: `latent_len`: all entries sum to 144. Every reader holds exactly two clips, with at most 16 latent frames between them; some reader holds exactly 16. An owner holds at most four clips and at most 18 latent frames; some owner holds four clips with 18 latent frames.
All inputs are finite; a program needn't handle non-finite values.
Results may differ from the reference program's by a relative error of at most 0.0046.
Values may be sent and summed in bfloat16 or wider, within the bound.
No kernel may reach another device: no remote copies, remote signals or barrier semaphores. Data moves between devices by JAX's collectives and lax.ppermute only.
A program may use at most 256 MiB of HBM per device.

```python
import jax
import jax.numpy as jnp
from jax import lax

C = 128
LAT = 16
LR = 4
GROUP_DEV = 9
PIX = 32
READ_F = 64
OWN_G = 18
GROUPS = 144
N_WIDE = 16


def plan_draw(key):
    wide_n = N_WIDE
    pair_count = wide_n // 2
    key_list = jax.random.split(jax.random.fold_in(key, 11), 7)
    tilt_by = jax.random.randint(key_list[0], (pair_count,), 0, GROUP_DEV - 2)
    forced = jax.random.randint(key_list[1], (), 0, pair_count)
    pair_ids = jnp.arange(pair_count)
    tilt_by = jnp.where(pair_ids == forced, GROUP_DEV - 2, tilt_by)
    totals = jnp.stack([GROUP_DEV + tilt_by, GROUP_DEV - tilt_by], axis=1).reshape(wide_n)
    low_len = jnp.maximum(1, totals - GROUP_DEV)
    high_len = jnp.minimum(GROUP_DEV, totals - 1)
    spread_draw = jax.random.randint(key_list[2], (wide_n,), 0, 1000)
    first_len = low_len + spread_draw % (high_len - low_len + 1)
    heavy_reader = jnp.arange(wide_n) == 2 * forced
    first_len = jnp.where(heavy_reader, high_len, first_len)
    slot_len = jnp.stack([first_len, totals - first_len], axis=1).reshape(2 * wide_n)
    reader_perm = jax.random.permutation(key_list[3], wide_n)
    clip_perm = jax.random.permutation(key_list[4], 2 * wide_n)
    owner_perm = jax.random.permutation(key_list[5], wide_n)
    slot_ids = jnp.arange(2 * wide_n)
    slot_reader = reader_perm[slot_ids // 2]
    owner_pick = jax.random.randint(key_list[6], (2 * wide_n,), 0, 2)
    owner_pick = jnp.where(slot_ids // 4 == forced, 0, owner_pick)
    slot_owner = owner_perm[2 * (slot_ids // 4) + owner_pick]
    latent_len = jnp.zeros((2 * wide_n,), jnp.int32).at[clip_perm].set(slot_len.astype(jnp.int32))
    reader = jnp.zeros((2 * wide_n,), jnp.int32).at[clip_perm].set(slot_reader.astype(jnp.int32))
    owner = jnp.zeros((2 * wide_n,), jnp.int32).at[clip_perm].set(slot_owner.astype(jnp.int32))
    return (latent_len, reader, owner)


def draw_latent_len(key, part):
    return plan_draw(key)[0]


def draw_reader(key, part):
    return plan_draw(key)[1]


def draw_owner(key, part):
    return plan_draw(key)[2]


def shard_levels(stream_key, shape, cuts, least, largest):
    level = 1.0
    for axis_at, shards_of in cuts:
        heights = jax.random.uniform(jax.random.fold_in(jax.random.fold_in(stream_key, 6), axis_at), (shards_of,), jnp.float32, least / len(cuts), largest / len(cuts))
        level = level * jnp.repeat(jnp.exp(heights), shape[axis_at] // shards_of).reshape((-1,) + (1,) * (len(shape) - 1 - axis_at))
    return level


def scatter_about(own_key, dims, scale, most, shards=(), kind=jnp.bfloat16):
    loudness = shard_levels(own_key, dims, shards, -0.22, 0.18) if shards else 1.0
    entries = jax.random.normal(own_key, dims, jnp.float32) * scale * loudness
    return jnp.minimum(jnp.maximum(entries, -most), most).astype(kind)


def setup_inputs(seed: int = 0, part: int = 0) -> dict:
    streams_of = jax.random.split(jax.random.key(seed), 13)
    own_keys = jax.random.split(jax.random.fold_in(streams_of[12], part), 13)
    frames = scatter_about(own_keys[0], (N_WIDE * READ_F, 3 * PIX * PIX), 1.0, 6.0, ((0, 16),))
    latent_len = draw_latent_len(jax.random.fold_in(jax.random.fold_in(streams_of[12], part), 71), part)
    reader = draw_reader(jax.random.fold_in(jax.random.fold_in(streams_of[12], part), 71), part)
    owner = draw_owner(jax.random.fold_in(jax.random.fold_in(streams_of[12], part), 71), part)
    w_in = scatter_about(streams_of[4], (C, 81), 81 ** -0.5, 0.625)
    b_in = scatter_about(streams_of[5], (C,), 0.5, 3.0, (), jnp.float32)
    g_in = jnp.clip(1.0 + 0.15 * jax.random.normal(streams_of[6], (C,), jnp.float32), 0.25, 1.75)
    w_down = scatter_about(streams_of[7], (C, 4 * C), (4 * C) ** -0.5, 0.25)
    b_down = scatter_about(streams_of[8], (C,), 0.5, 3.0, (), jnp.float32)
    g_down = jnp.clip(1.0 + 0.15 * jax.random.normal(streams_of[9], (C,), jnp.float32), 0.25, 1.75)
    w_head = scatter_about(streams_of[10], (LAT, 64 * C), (64 * C) ** -0.5, 0.0625)
    b_head = scatter_about(streams_of[11], (LAT,), 0.5, 3.0, (), jnp.float32)
    return dict(frames=frames, latent_len=latent_len, reader=reader, owner=owner, w_in=w_in, b_in=b_in, g_in=g_in, w_down=w_down, b_down=b_down, g_down=g_down, w_head=w_head, b_head=b_head)


epsilon = 1e-06

def clip_tables(latent_len, reader, owner):
    clip_count = latent_len.shape[0]
    clip_range = jnp.arange(clip_count, dtype=jnp.int32)
    earlier = clip_range[None, :] < clip_range[:, None]
    frame_len = 4 * latent_len - 3
    same_reader = reader[None, :] == reader[:, None]
    same_owner = owner[None, :] == owner[:, None]
    read_off = lax.optimization_barrier(jnp.sum(jnp.where(earlier & same_reader, frame_len[None, :], 0), axis=1)).astype(jnp.int32)
    own_off = lax.optimization_barrier(jnp.sum(jnp.where(earlier & same_owner, latent_len[None, :], 0), axis=1)).astype(jnp.int32)
    order_key = reader * clip_count + clip_range
    before = order_key[None, :] < order_key[:, None]
    deal_start = lax.optimization_barrier(jnp.sum(jnp.where(before, latent_len[None, :], 0), axis=1)).astype(jnp.int32)
    return (read_off, own_off, deal_start)

def find_clip(group_ids, deal_start, latent_len):
    clip_range = jnp.arange(latent_len.shape[0], dtype=jnp.int32)
    inside = (deal_start[None, :] <= group_ids[:, None]) & (group_ids[:, None] < (deal_start + latent_len)[None, :])
    clip_ids = lax.optimization_barrier(jnp.sum(jnp.where(inside, clip_range[None, :], 0), axis=1)).astype(jnp.int32)
    present = jnp.any(inside, axis=1)
    latent_idx = (group_ids - deal_start[clip_ids]).astype(jnp.int32)
    return (clip_ids, latent_idx, present)

def frame_index(latent_idx):
    slot_ids = jnp.arange(6, dtype=jnp.int32)
    later = 4 * latent_idx[:, None] - 5 + slot_ids[None, :]
    opening = jnp.broadcast_to(slot_ids[None, :] - 5, later.shape)
    return jnp.where(latent_idx[:, None] > 0, later, opening).astype(jnp.int32)

def norm_silu(values, gain_vec):
    mean_square = lax.optimization_barrier(jnp.mean(values * values, axis=0, keepdims=True))
    return jax.nn.silu(values * lax.rsqrt(mean_square + epsilon) * gain_vec[:, None])

def encode_group(block, opening, weights):
    w_in, b_in, g_in, w_down, b_down, g_down, w_head, b_head = weights
    channels = w_in.shape[0]
    picture = block.reshape(6, 3, PIX, PIX)
    padded = jnp.pad(picture, ((0, 0), (0, 0), (1, 1), (1, 1)))
    shifted = jnp.stack([padded[:, :, row_off:row_off + PIX, col_off:col_off + PIX] for row_off in range(3) for col_off in range(3)], axis=1)
    shifted = shifted.reshape(6, 27, PIX * PIX)
    reduced_list = []
    for frame_slot in range(4):
        columns = shifted[frame_slot:frame_slot + 3].reshape(81, PIX * PIX)
        convolved = jnp.dot(w_in, columns, preferred_element_type=jnp.float32) + b_in[:, None]
        full_res = norm_silu(convolved, g_in).astype(jnp.bfloat16)
        merged = full_res.reshape(channels, PIX // 2, 2, PIX // 2, 2).transpose(0, 2, 4, 1, 3).reshape(4 * channels, PIX // 2 * (PIX // 2))
        lowered = jnp.dot(w_down, merged, preferred_element_type=jnp.float32) + b_down[:, None]
        reduced = norm_silu(lowered, g_down).astype(jnp.bfloat16)
        if frame_slot < 3:
            reduced = jnp.where(opening, jnp.zeros_like(reduced), reduced)
        reduced_list.append(reduced)
    stacked = jnp.stack(reduced_list).reshape(4, channels, LR, 4, LR, 4).transpose(0, 1, 3, 5, 2, 4).reshape(64 * channels, LR * LR)
    latent = jnp.dot(w_head, stacked, preferred_element_type=jnp.float32) + b_head[:, None]
    return latent.reshape(-1).astype(jnp.bfloat16)

def reference(frames, latent_len, reader, owner, w_in, b_in, g_in, w_down, b_down, g_down, w_head, b_head):
    weights = (w_in, b_in, g_in, w_down, b_down, g_down, w_head, b_head)
    read_off, own_off, deal_start = clip_tables(latent_len, reader, owner)
    group_ids = jnp.arange(GROUPS, dtype=jnp.int32)
    clip_ids, latent_idx, present = find_clip(group_ids, deal_start, latent_len)
    frame_ids = frame_index(latent_idx)
    live = frame_ids >= 0
    row_ids = (reader[clip_ids] * READ_F + read_off[clip_ids]).astype(jnp.int32)[:, None] + jnp.maximum(frame_ids, 0)
    blocks = jnp.where(live[:, :, None], frames[row_ids], jnp.zeros((), frames.dtype))
    encoded = lax.map(lambda packed: encode_group(packed[0], packed[1], weights), (blocks, latent_idx == 0))
    out_rows = (owner[clip_ids] * OWN_G + own_off[clip_ids] + latent_idx).astype(jnp.int32)
    result = jnp.zeros((N_WIDE * OWN_G, encoded.shape[1]), encoded.dtype)
    return result.at[out_rows].set(encoded)
```

```python
import functools

import jax
import jax.numpy as jnp
import numpy as np
from jax import lax
from jax.experimental import pallas as pl
from jax.experimental.pallas import tpu as pltpu
from jax.sharding import PartitionSpec as P

PIX = 32
EPS = 1e-06
TAP = 48
DEPTH = 160
F32 = jnp.float32
BF16 = jnp.bfloat16


def patch_spread():
    spread = np.zeros((4, 81, DEPTH), np.float32)
    for a2 in range(2):
        for b2 in range(2):
            for t in range(3):
                for a in range(3):
                    for b in range(3):
                        for k in range(3):
                            row = t * 27 + (a * 3 + b) * 3 + k
                            col = t * TAP + k * 16 + (a2 + a) * 4 + b2 + b
                            spread[2 * a2 + b2, row, col] = 1
    return jnp.asarray(spread, BF16)


def iota(shape, axis):
    return lax.broadcasted_iota(jnp.int32, shape, axis)


def one_hot(flags):
    return jnp.where(flags, 1.0, 0.0).astype(BF16)


def dot(a, b):
    return jnp.dot(a, b, preferred_element_type=F32)


def column(row):
    n = row.shape[1]
    eye = iota((n, n), 0) == iota((n, n), 1)
    return jnp.sum(jnp.where(eye, row, 0.0), axis=1, keepdims=True)


def half_silu_norm(values, half_gain):
    mean_square = jnp.sum(values * values, axis=0, keepdims=True) * (1.0 / values.shape[0])
    h = values * lax.rsqrt(mean_square + EPS) * half_gain
    return (h + h * jnp.tanh(h)).astype(BF16)


def pick_rows(me, steps, rows, own_rows, len_row, reader_row, owner_row):
    clips = len_row.shape[1]
    lens = len_row.astype(F32)
    len_col = column(lens)
    reader_col = column(reader_row.astype(F32))
    owner_col = column(owner_row.astype(F32))
    earlier = iota((clips, clips), 0) < iota((clips, clips), 1)
    same_reader = reader_col == reader_row.astype(F32)
    same_owner = owner_col == owner_row.astype(F32)
    read_off = jnp.sum(jnp.where(earlier & same_reader, len_col, 0.0), axis=0, keepdims=True)
    own_off = jnp.sum(jnp.where(earlier & same_owner, len_col, 0.0), axis=0, keepdims=True)
    away = reader_row ^ me
    block = jnp.zeros_like(away)
    for at, step in enumerate(steps):
        block = block + jnp.where((away & step) != 0, 1 << at, 0)
    slot = iota((own_rows, clips), 0).astype(F32)
    inside = (owner_row == me) & (own_off <= slot) & (slot < own_off + lens)
    source = block.astype(F32) * rows + read_off - own_off + slot
    source = jnp.sum(jnp.where(inside, source + 1.0, 0.0), axis=1, keepdims=True) - 1.0
    width = rows << len(steps)
    return one_hot(iota((own_rows, width), 1).astype(F32) == source)


def encode_kernel(
    steps,
    len_s,
    reader_s,
    frames,
    len_row,
    reader_row,
    owner_row,
    spread,
    w_in,
    b_in,
    g_in,
    w_down,
    b_down,
    g_down,
    w_head,
    b_head,
    latents,
    pick,
    raw,
    patches,
    wide_in,
    wide_down,
    wide_head,
    gain_in,
    gain_down,
    bias_down,
    partial,
):
    me = lax.axis_index("wide")
    read_rows = frames.shape[0]
    clips = len_s.shape[0]
    rows = latents.shape[0]

    len0 = jnp.int32(0)
    len1 = jnp.int32(0)
    for c in range(clips):
        mine = reader_s[c] == me
        length = len_s[c]
        len1 = jnp.where(mine & (len0 > 0), length, len1)
        len0 = jnp.where(mine & (len0 == 0), length, len0)
    frames0 = 4 * len0 - 3

    pick[...] = pick_rows(
        me, steps, rows, pick.shape[0], len_row[...], reader_row[...], owner_row[...]
    )

    gain_in[...] = jnp.broadcast_to(column(g_in[...]) * 0.5, gain_in.shape)
    gain_down[...] = jnp.broadcast_to(column(g_down[...]) * 0.5, gain_down.shape)
    bias_down[...] = jnp.broadcast_to(column(b_down[...]), bias_down.shape)
    bias = column(b_in[...])
    bias_high = bias.astype(BF16).astype(F32)
    bias_mid = (bias - bias_high).astype(BF16).astype(F32)
    bias_low = bias - bias_high - bias_mid
    lane = iota((128, DEPTH), 1)
    bias_lanes = jnp.where(
        lane == 144,
        bias_high,
        jnp.where(lane == 145, bias_mid, jnp.where(lane == 146, bias_low, 0.0)),
    )
    for p in range(4):
        wide_in[p * 128 : (p + 1) * 128, :] = (dot(w_in[...], spread[p]) + bias_lanes).astype(BF16)
    source = iota((512, 512), 0)
    order = one_hot((source % 4) * 128 + source // 4 == iota((512, 512), 1))
    wide_down[...] = dot(w_down[...], order).astype(BF16)
    source = iota((256, 256), 0)
    order = one_hot((source % 16) * 16 + source // 16 == iota((256, 256), 1))
    chunks = []
    for chunk in range(8):
        piece = jnp.concatenate(
            [w_head[:, s * 2048 + chunk * 256 : s * 2048 + (chunk + 1) * 256] for s in range(4)],
            axis=0,
        )
        chunks.append(dot(piece, order))
    group = iota((64, 128), 1) // 16
    for half in range(2):
        parts = [chunk[:, half * 128 : (half + 1) * 128] for chunk in chunks]
        for bit in (1, 2, 4):
            upper = (group & bit) != 0
            for i in range(8):
                if i & bit:
                    continue
                low, high = parts[i], parts[i | bit]
                parts[i] = jnp.where(upper, pltpu.roll(high, bit * 16, 1), low)
                parts[i | bit] = jnp.where(upper, high, pltpu.roll(low, 128 - bit * 16, 1))
        for i in range(8):
            at = (half * 8 + i) * 16
            for s in range(4):
                wide_head[at : at + 16, s * 128 : (s + 1) * 128] = parts[i][
                    s * 16 : (s + 1) * 16
                ].astype(BF16)

    source = iota((512, 512), 0)
    line, pix = source // PIX, source % PIX
    target = ((line % 2) * 2 + pix % 2) * 128 + (line // 2) * 16 + pix // 2
    order = one_hot(target == iota((512, 512), 1))
    split = []
    for h in range(2):
        piece = jnp.concatenate(
            [frames[:, k * 1024 + h * 512 : k * 1024 + (h + 1) * 512] for k in range(3)], axis=0
        )
        split.append(dot(piece, order))
    square = iota((read_rows, 256), 1)
    up, across = square // 16, square % 16
    for k in range(3):
        for r in range(4):
            for s in range(4):
                p = ((r + 1) % 2) * 2 + (s + 1) % 2
                values = jnp.concatenate(
                    [
                        part[k * read_rows : (k + 1) * read_rows, p * 128 : (p + 1) * 128]
                        for part in split
                    ],
                    axis=1,
                )
                dy, dx = (-1, 0, 0, 1)[r], (-1, 0, 0, 1)[s]
                shift = (-(dy * 16 + dx)) % 256
                if shift:
                    values = pltpu.roll(values, shift, 1)
                    good = None
                    for d, place in ((dy, up), (dx, across)):
                        if d:
                            ok = place > 0 if d < 0 else place < 15
                            good = ok if good is None else good & ok
                    values = jnp.where(good, values, 0.0)
                at = (k * 16 + r * 4 + s) * read_rows
                for h in range(2):
                    raw[h, at : at + read_rows, :] = values[:, h * 128 : (h + 1) * 128]

    def place(frame, carry):
        slot = frame + 2 + jnp.where(frame >= frames0, 2, 0)
        to = pl.multiple_of(slot * TAP, TAP)
        for h in range(2):
            patches[pl.ds(to, TAP), h * 128 : (h + 1) * 128] = raw[
                h, pl.ds(frame, TAP, stride=read_rows), :
            ].astype(BF16)
        return carry

    lax.fori_loop(0, read_rows, place, 0, unroll=4)
    blank = jnp.zeros((2 * TAP, 256), BF16)
    patches[: 2 * TAP, :] = blank
    patches[pl.ds(pl.multiple_of((frames0 + 2) * TAP, TAP), 2 * TAP), :] = blank

    square = iota((1, 256), 1)
    corner = (square // 16 % 4) * 4 + square % 4
    ones = jnp.ones((16, 256), BF16)

    def reduce_frame(slot, opening=False):
        if opening:
            taps = patches[pl.ds(pl.multiple_of(slot * TAP, TAP), TAP), :]
            columns = jnp.concatenate([blank, taps, ones], axis=0)
        else:
            taps = patches[pl.ds(pl.multiple_of((slot - 2) * TAP, TAP), 3 * TAP), :]
            columns = jnp.concatenate([taps, ones], axis=0)
        merged = jnp.concatenate(
            [
                half_silu_norm(dot(wide_in[p * 128 : (p + 1) * 128, :], columns), gain_in[...])
                for p in range(4)
            ],
            axis=0,
        )
        lowered = dot(wide_down[...], merged) + bias_down[...]
        return half_silu_norm(lowered, gain_down[...])

    def keep(row, product):
        total = jnp.zeros((16, 256), F32)
        for ab in range(16):
            total = total + jnp.where(corner == ab, product[ab * 16 : (ab + 1) * 16], 0.0)
        partial[pl.ds(pl.multiple_of(row * 16, 16), 16), :] = total

    partial[...] = jnp.zeros_like(partial)
    def opening(c, carry):
        keep(c * len0, dot(wide_head[:, 384:], reduce_frame(2 + c * (frames0 + 2), True)))
        return carry

    lax.fori_loop(0, 2, opening, 0)

    def later(i, carry):
        second = i >= len0 - 1
        j = i + 1 - jnp.where(second, len0 - 1, 0)
        first = 4 * j - 3 + 2 + jnp.where(second, frames0 + 2, 0)
        row = j + jnp.where(second, len0, 0)
        reduced = jnp.concatenate([reduce_frame(first + s) for s in range(4)], axis=0)
        keep(row, dot(wide_head[...], reduced))
        return carry

    lax.fori_loop(0, len0 + len1 - 2, later, 0)

    place_of = iota((256, 256), 0)
    cell = (place_of // 64) * 4 + place_of % 16 // 4
    sums = jnp.where(cell == iota((256, 256), 1) % 16, 1.0, 0.0)
    spots = jnp.dot(
        partial[...], sums, precision=lax.Precision.HIGHEST, preferred_element_type=F32
    )
    channel = iota((16, 256), 1) // 16 == iota((16, 256), 0)
    bias = jnp.sum(jnp.where(channel, column(b_head[...]), 0.0), axis=0, keepdims=True)
    spots = jnp.where(channel[None], spots.reshape(rows, 16, 256), 0.0)
    latents[...] = (jnp.sum(spots, axis=1) + bias).astype(BF16)


def encode(steps, own_rows, rows, frames, latent_len, reader, owner, weights):
    w_in, b_in, g_in, w_down, b_down, g_down, w_head, b_head = weights
    read_rows = frames.shape[0]
    vmem = pl.BlockSpec(memory_space=pltpu.VMEM)
    smem = pl.BlockSpec(memory_space=pltpu.SMEM)
    row = lambda x: x.reshape(1, -1)
    return pl.pallas_call(
        functools.partial(encode_kernel, steps),
        out_shape=(
            jax.ShapeDtypeStruct((rows, 256), BF16),
            jax.ShapeDtypeStruct((own_rows, rows << len(steps)), BF16),
        ),
        in_specs=[smem, smem] + [vmem] * 13,
        out_specs=(vmem, vmem),
        scratch_shapes=[
            pltpu.VMEM((2, read_rows * TAP, 128), F32),
            pltpu.VMEM(((read_rows + 4) * TAP, 256), BF16),
            pltpu.VMEM((512, DEPTH), BF16),
            pltpu.VMEM((128, 512), BF16),
            pltpu.VMEM((256, 512), BF16),
            pltpu.VMEM((128, 256), F32),
            pltpu.VMEM((128, 256), F32),
            pltpu.VMEM((128, 256), F32),
            pltpu.VMEM((rows * 16, 256), F32),
        ],
    )(
        latent_len,
        reader,
        frames,
        row(latent_len),
        row(reader),
        row(owner),
        patch_spread(),
        w_in,
        row(b_in),
        row(g_in),
        w_down,
        row(b_down),
        row(g_down),
        w_head,
        row(b_head),
    )


def shards(
    frames, latent_len, reader, owner, w_in, b_in, g_in, w_down, b_down, g_down, w_head, b_head
):
    weights = (w_in, b_in, g_in, w_down, b_down, g_down, w_head, b_head)
    wide_n = lax.axis_size("wide")
    steps = []
    step = wide_n // 2
    while step:
        steps.append(step)
        step //= 2
    most_read = frames.shape[0] // 4
    own_rows = 2 * ((most_read + 2) // 2)
    rows = -(-most_read // 16) * 16
    latents, pick = encode(steps, own_rows, rows, frames, latent_len, reader, owner, weights)
    for step in steps:
        pairs = [(i, i ^ step) for i in range(wide_n)]
        latents = jnp.concatenate([latents, lax.ppermute(latents, "wide", pairs)], axis=0)
    return jnp.dot(pick, latents, preferred_element_type=F32).astype(BF16)


def solution(mesh):
    return jax.shard_map(
        shards,
        mesh=mesh,
        in_specs=(P(("groups", "wide"), None), P("groups"), P("groups"), P("groups")) + (P(),) * 8,
        out_specs=P(("groups", "wide"), None),
        check_vma=False,
    )
```

```python
import functools

import jax
import jax.numpy as jnp
import numpy as np
from jax import lax
from jax.experimental import pallas as pl
from jax.experimental.pallas import tpu as pltpu
from jax.sharding import PartitionSpec as P

PIX = 32
EPS = 1e-06
TAP = 48
DEPTH = 160
F32 = jnp.float32
BF16 = jnp.bfloat16


def patch_spread():
    spread = np.zeros((4, 81, DEPTH), np.float32)
    for a2 in range(2):
        for b2 in range(2):
            for t in range(3):
                for a in range(3):
                    for b in range(3):
                        for k in range(3):
                            row = t * 27 + (a * 3 + b) * 3 + k
                            col = t * TAP + k * 16 + (a2 + a) * 4 + b2 + b
                            spread[2 * a2 + b2, row, col] = 1
    return jnp.asarray(spread, BF16)


def iota(shape, axis):
    return lax.broadcasted_iota(jnp.int32, shape, axis)


def one_hot(flags):
    return jnp.where(flags, 1.0, 0.0).astype(BF16)


def dot(a, b):
    return jnp.dot(a, b, preferred_element_type=F32)


def twice(x):
    return jnp.concatenate([x, x], axis=1)


def arrangement(size, move):
    to = move(iota((size, 128), 0))
    lane = iota((size, 128), 1)
    return jnp.concatenate([one_hot(to == lane + at) for at in range(0, size, 128)], axis=1)


def column(row):
    n = row.shape[1]
    eye = iota((n, n), 0) == iota((n, n), 1)
    return jnp.sum(jnp.where(eye, row, 0.0), axis=1, keepdims=True)


def half_silu_norm(values, half_gain, narrow):
    mean_square = jnp.sum(values * values, axis=0, keepdims=True) * (1.0 / values.shape[0])
    h = values * lax.rsqrt(mean_square + EPS) * half_gain
    if narrow:
        h = h.astype(BF16)
    return (h + h * jnp.tanh(h)).astype(BF16)


def pick_rows(me, steps, rows, own_rows, len_row, reader_row, owner_row):
    clips = len_row.shape[1]
    lens = len_row.astype(F32)
    len_col = column(lens)
    reader_col = column(reader_row.astype(F32))
    owner_col = column(owner_row.astype(F32))
    earlier = iota((clips, clips), 0) < iota((clips, clips), 1)
    same_reader = reader_col == reader_row.astype(F32)
    same_owner = owner_col == owner_row.astype(F32)
    read_off = jnp.sum(jnp.where(earlier & same_reader, len_col, 0.0), axis=0, keepdims=True)
    own_off = jnp.sum(jnp.where(earlier & same_owner, len_col, 0.0), axis=0, keepdims=True)
    away = reader_row ^ me
    block = jnp.zeros_like(away)
    for at, step in enumerate(steps):
        block = block + jnp.where((away & step) != 0, 1 << at, 0)
    slot = iota((own_rows, clips), 0).astype(F32)
    inside = (owner_row == me) & (own_off <= slot) & (slot < own_off + lens)
    source = block.astype(F32) * rows + read_off - own_off + slot
    source = jnp.sum(jnp.where(inside, source + 1.0, 0.0), axis=1, keepdims=True) - 1.0
    width = rows << len(steps)
    return one_hot(iota((own_rows, width), 1).astype(F32) == source)


def encode_kernel(
    steps,
    len_s,
    reader_s,
    frames,
    len_row,
    reader_row,
    owner_row,
    spread,
    w_in,
    b_in,
    g_in,
    w_down,
    b_down,
    g_down,
    w_head,
    b_head,
    latents,
    pick,
    raw,
    patches,
    wide_in,
    wide_down,
    wide_head,
    gain_in,
    gain_down,
    bias_down,
    partial,
    merged,
):
    me = lax.axis_index("wide")
    read_rows = frames.shape[0]
    clips = len_s.shape[0]
    rows = latents.shape[0]

    len0 = jnp.int32(0)
    len1 = jnp.int32(0)
    for c in range(clips):
        mine = reader_s[c] == me
        length = len_s[c]
        len1 = jnp.where(mine & (len0 > 0), length, len1)
        len0 = jnp.where(mine & (len0 == 0), length, len0)
    frames0 = 4 * len0 - 3

    pick[...] = pick_rows(
        me, steps, rows, pick.shape[0], len_row[...], reader_row[...], owner_row[...]
    )

    gain_in[...] = jnp.broadcast_to(column(g_in[...]) * 0.5, gain_in.shape)
    gain_down[...] = jnp.broadcast_to(column(g_down[...]) * 0.5, gain_down.shape)
    bias_down[...] = jnp.broadcast_to(column(b_down[...]), bias_down.shape)
    bias = column(b_in[...])
    bias_high = bias.astype(BF16).astype(F32)
    bias_mid = (bias - bias_high).astype(BF16).astype(F32)
    bias_low = bias - bias_high - bias_mid
    lane = iota((128, DEPTH), 1)
    bias_lanes = jnp.where(
        lane == 144,
        bias_high,
        jnp.where(lane == 145, bias_mid, jnp.where(lane == 146, bias_low, 0.0)),
    )
    for p in range(4):
        taps = lax.dot_general(
            w_in[...], spread[p], (((0,), (0,)), ((), ())), preferred_element_type=F32
        )
        wide_in[p * 128 : (p + 1) * 128, :] = (taps + bias_lanes).astype(BF16)
    order = arrangement(512, lambda i: ((i & 3) << 7) | (i >> 2))
    wide_down[...] = dot(w_down[...], order).astype(BF16)
    order = arrangement(256, lambda i: ((i & 15) << 4) | (i >> 4))
    chunks = []
    for chunk in range(8):
        piece = jnp.concatenate(
            [w_head[:, s * 2048 + chunk * 256 : s * 2048 + (chunk + 1) * 256] for s in range(4)],
            axis=0,
        )
        chunks.append(dot(piece, order))
    group = iota((64, 128), 1) >> 4
    for half in range(2):
        parts = [chunk[:, half * 128 : (half + 1) * 128] for chunk in chunks]
        for bit in (1, 2, 4):
            upper = (group & bit) != 0
            for i in range(8):
                if i & bit:
                    continue
                low, high = parts[i], parts[i | bit]
                parts[i] = jnp.where(upper, pltpu.roll(high, bit * 16, 1), low)
                parts[i | bit] = jnp.where(upper, high, pltpu.roll(low, 128 - bit * 16, 1))
        for i in range(8):
            at = (half * 8 + i) * 16
            for s in range(4):
                wide_head[at : at + 16, s * 128 : (s + 1) * 128] = parts[i][
                    s * 16 : (s + 1) * 16
                ].astype(BF16)

    order = arrangement(
        512,
        lambda i: ((i & 32) << 3) | ((i & 1) << 7) | ((i & 448) >> 2) | ((i & 30) >> 1),
    )
    split = []
    for h in range(2):
        piece = jnp.concatenate(
            [frames[:, k * 1024 + h * 512 : k * 1024 + (h + 1) * 512] for k in range(3)], axis=0
        )
        split.append(dot(piece, order))
    square = iota((read_rows, 256), 1)
    up, across = square >> 4, square & 15
    for k in range(3):
        for r in range(4):
            for s in range(4):
                p = ((r + 1) % 2) * 2 + (s + 1) % 2
                values = jnp.concatenate(
                    [
                        part[k * read_rows : (k + 1) * read_rows, p * 128 : (p + 1) * 128]
                        for part in split
                    ],
                    axis=1,
                )
                dy, dx = (-1, 0, 0, 1)[r], (-1, 0, 0, 1)[s]
                shift = (-(dy * 16 + dx)) % 256
                if shift:
                    values = pltpu.roll(values, shift, 1)
                    good = None
                    for d, place in ((dy, up), (dx, across)):
                        if d:
                            ok = place > 0 if d < 0 else place < 15
                            good = ok if good is None else good & ok
                    values = jnp.where(good, values, 0.0)
                at = (k * 16 + r * 4 + s) * (read_rows + 1)
                for h in range(2):
                    raw[h, at : at + read_rows, :] = values[:, h * 128 : (h + 1) * 128]

    def place(frame, carry):
        slot = frame + 2 + jnp.where(frame >= frames0, 2, 0)
        to = pl.multiple_of(slot * TAP, TAP)
        for h in range(2):
            patches[pl.ds(to, TAP), h * 128 : (h + 1) * 128] = raw[
                h, pl.ds(frame, TAP, stride=read_rows + 1), :
            ].astype(BF16)
        return carry

    lax.fori_loop(0, read_rows, place, 0, unroll=4)
    blank = jnp.zeros((2 * TAP, 256), BF16)
    patches[: 2 * TAP, :] = blank
    patches[pl.ds(pl.multiple_of((frames0 + 2) * TAP, TAP), 2 * TAP), :] = blank

    square = iota((1, 256), 1)
    corner = ((square >> 4 & 3) << 2) | (square & 3)
    ones = jnp.ones((16, 256), BF16)

    def convolve(columns):
        return jnp.concatenate(
            [
                half_silu_norm(dot(wide_in[p * 128 : (p + 1) * 128, :], columns), twice(gain_in[...]), False)
                for p in range(4)
            ],
            axis=0,
        )

    def lower(columns):
        return half_silu_norm(
            dot(wide_down[...], columns) + twice(bias_down[...]), twice(gain_down[...]), False
        )

    def keep(row, product):
        total = jnp.zeros((16, 256), F32)
        for ab in range(16):
            total = total + jnp.where(corner == ab, product[ab * 16 : (ab + 1) * 16], 0.0)
        partial[pl.ds(pl.multiple_of(row * 16, 16), 16), :] = total

    partial[...] = jnp.zeros_like(partial)

    def opening(c, carry):
        slot = 2 + c * (frames0 + 2)
        taps = patches[pl.ds(pl.multiple_of(slot * TAP, TAP), TAP), :]
        columns = jnp.concatenate([blank, taps, ones], axis=0)
        keep(c * len0, dot(wide_head[:, 384:], lower(convolve(columns))))
        return carry

    lax.fori_loop(0, 2, opening, 0)

    count = len0 + len1 - 2

    def columns_of(frame):
        taps = patches[pl.ds(pl.multiple_of(frame * TAP, TAP), 3 * TAP), :]
        return jnp.concatenate([taps, ones], axis=0)

    def first_frame(i):
        second = i >= len0 - 1
        j = i + 1 - jnp.where(second, len0 - 1, 0)
        return 4 * j - 3 + jnp.where(second, frames0 + 2, 0)

    def first_half(i):
        first = first_frame(i)
        for s in range(4):
            merged[s] = convolve(columns_of(first + s))

    def second_half(i):
        row = i + 1 + jnp.where(i >= len0 - 1, 1, 0)
        reduced = jnp.concatenate([lower(merged[s]) for s in range(4)], axis=0)
        keep(row, dot(wide_head[...], reduced))

    @pl.when(count > 0)
    def _():
        first_half(0)

    def both(i, carry):
        second_half(i)
        first_half(i + 1)
        return carry

    lax.fori_loop(0, count - 1, both, 0)

    @pl.when(count > 0)
    def _():
        second_half(count - 1)

    place_of = iota((256, 128), 0)
    cell = ((place_of >> 6) << 2) | ((place_of & 15) >> 2)
    sums = one_hot(cell == (iota((256, 128), 1) & 15))
    sums = jnp.concatenate([sums, sums], axis=1)
    high = partial[...].astype(BF16)
    spots = dot(high, sums) + dot((partial[...] - high.astype(F32)).astype(BF16), sums)
    channel = (iota((16, 256), 1) >> 4) == iota((16, 256), 0)
    bias = jnp.sum(jnp.where(channel, column(b_head[...]), 0.0), axis=0, keepdims=True)
    spots = jnp.where(channel[None], spots.reshape(rows, 16, 256), 0.0)
    latents[...] = (jnp.sum(spots, axis=1) + bias).astype(BF16)


def encode(steps, own_rows, rows, frames, latent_len, reader, owner, weights):
    w_in, b_in, g_in, w_down, b_down, g_down, w_head, b_head = weights
    read_rows = frames.shape[0]
    vmem = pl.BlockSpec(memory_space=pltpu.VMEM)
    smem = pl.BlockSpec(memory_space=pltpu.SMEM)
    row = lambda x: x.reshape(1, -1)
    return pl.pallas_call(
        functools.partial(encode_kernel, steps),
        out_shape=(
            jax.ShapeDtypeStruct((rows, 256), BF16),
            jax.ShapeDtypeStruct((own_rows, rows << len(steps)), BF16),
        ),
        in_specs=[smem, smem] + [vmem] * 13,
        out_specs=(vmem, vmem),
        scratch_shapes=[
            pltpu.VMEM((2, (read_rows + 1) * TAP, 128), F32),
            pltpu.VMEM(((read_rows + 4) * TAP, 256), BF16),
            pltpu.VMEM((512, DEPTH), BF16),
            pltpu.VMEM((128, 512), BF16),
            pltpu.VMEM((256, 512), BF16),
            pltpu.VMEM((128, 128), F32),
            pltpu.VMEM((128, 128), F32),
            pltpu.VMEM((128, 128), F32),
            pltpu.VMEM((rows * 16, 256), F32),
            pltpu.VMEM((4, 512, 256), BF16),
        ],
    )(
        latent_len,
        reader,
        frames,
        row(latent_len),
        row(reader),
        row(owner),
        patch_spread(),
        w_in.T,
        row(b_in),
        row(g_in),
        w_down,
        row(b_down),
        row(g_down),
        w_head,
        row(b_head),
    )


def shards(
    frames, latent_len, reader, owner, w_in, b_in, g_in, w_down, b_down, g_down, w_head, b_head
):
    weights = (w_in, b_in, g_in, w_down, b_down, g_down, w_head, b_head)
    wide_n = lax.axis_size("wide")
    steps = []
    step = wide_n // 2
    while step:
        steps.append(step)
        step //= 2
    most_read = frames.shape[0] // 4
    own_rows = 2 * ((most_read + 2) // 2)
    rows = -(-most_read // 16) * 16
    latents, pick = encode(steps, own_rows, rows, frames, latent_len, reader, owner, weights)
    for step in steps:
        pairs = [(i, i ^ step) for i in range(wide_n)]
        latents = jnp.concatenate([latents, lax.ppermute(latents, "wide", pairs)], axis=0)
    return jnp.dot(pick, latents, preferred_element_type=F32).astype(BF16)


def solution(mesh):
    return jax.shard_map(
        shards,
        mesh=mesh,
        in_specs=(P(("groups", "wide"), None), P("groups"), P("groups"), P("groups")) + (P(),) * 8,
        out_specs=P(("groups", "wide"), None),
        check_vma=False,
    )
```

```python
import functools

import jax
import jax.numpy as jnp
import numpy as np
from jax import lax
from jax.experimental import pallas as pl
from jax.experimental.pallas import tpu as pltpu
from jax.sharding import PartitionSpec as P

PIX = 32
EPS = 1e-06
TAP = 48
DEPTH = 160
F32 = jnp.float32
BF16 = jnp.bfloat16


def patch_spread():
    spread = np.zeros((4, 81, DEPTH), np.float32)
    for a2 in range(2):
        for b2 in range(2):
            for t in range(3):
                for a in range(3):
                    for b in range(3):
                        for k in range(3):
                            row = t * 27 + (a * 3 + b) * 3 + k
                            col = t * TAP + k * 16 + (a2 + a) * 4 + b2 + b
                            spread[2 * a2 + b2, row, col] = 1
    return jnp.asarray(spread, BF16)


def iota(shape, axis):
    return lax.broadcasted_iota(jnp.int32, shape, axis)


def one_hot(flags):
    return jnp.where(flags, 1.0, 0.0).astype(BF16)


def dot(a, b):
    return jnp.dot(a, b, preferred_element_type=F32)


def twice(x):
    return jnp.concatenate([x, x], axis=1)


def arrangement(size, move):
    to = move(iota((size, 128), 0))
    lane = iota((size, 128), 1)
    return jnp.concatenate([one_hot(to == lane + at) for at in range(0, size, 128)], axis=1)


def column(row):
    n = row.shape[1]
    eye = iota((n, n), 0) == iota((n, n), 1)
    return jnp.sum(jnp.where(eye, row, 0.0), axis=1, keepdims=True)


def half_silu_norm(values, half_gain, narrow):
    mean_square = jnp.sum(values * values, axis=0, keepdims=True) * (1.0 / values.shape[0])
    h = values * lax.rsqrt(mean_square + EPS) * half_gain
    if narrow:
        h = h.astype(BF16)
    return (h + h * jnp.tanh(h)).astype(BF16)


def pick_rows(me, steps, rows, own_rows, len_row, reader_row, owner_row):
    clips = len_row.shape[1]
    lens = len_row.astype(F32)
    len_col = column(lens)
    reader_col = column(reader_row.astype(F32))
    owner_col = column(owner_row.astype(F32))
    earlier = iota((clips, clips), 0) < iota((clips, clips), 1)
    same_reader = reader_col == reader_row.astype(F32)
    same_owner = owner_col == owner_row.astype(F32)
    read_off = jnp.sum(jnp.where(earlier & same_reader, len_col, 0.0), axis=0, keepdims=True)
    own_off = jnp.sum(jnp.where(earlier & same_owner, len_col, 0.0), axis=0, keepdims=True)
    away = reader_row ^ me
    block = jnp.zeros_like(away)
    for at, step in enumerate(steps):
        block = block + jnp.where((away & step) != 0, 1 << at, 0)
    slot = iota((own_rows, clips), 0).astype(F32)
    inside = (owner_row == me) & (own_off <= slot) & (slot < own_off + lens)
    source = block.astype(F32) * rows + read_off - own_off + slot
    source = jnp.sum(jnp.where(inside, source + 1.0, 0.0), axis=1, keepdims=True) - 1.0
    width = rows << len(steps)
    return one_hot(iota((own_rows, width), 1).astype(F32) == source)


def encode_kernel(
    steps,
    len_s,
    reader_s,
    frames_hbm,
    len_row_hbm,
    reader_row_hbm,
    owner_row_hbm,
    spread_hbm,
    w_in_hbm,
    b_in_hbm,
    g_in_hbm,
    w_down_hbm,
    b_down_hbm,
    g_down_hbm,
    w_head_hbm,
    b_head_hbm,
    latents,
    pick,
    raw,
    patches,
    wide_in,
    wide_down,
    wide_head,
    gain_in,
    gain_down,
    bias_down,
    partial,
    merged,
    frames,
    len_row,
    reader_row,
    owner_row,
    spread,
    w_in,
    b_in,
    g_in,
    w_down,
    b_down,
    g_down,
    w_head,
    b_head,
    arrived,
):
    fetches = {}
    for n, (source, target) in enumerate(
        (
            (frames_hbm, frames),
            (len_row_hbm, len_row),
            (reader_row_hbm, reader_row),
            (owner_row_hbm, owner_row),
            (spread_hbm, spread),
            (w_in_hbm, w_in),
            (b_in_hbm, b_in),
            (g_in_hbm, g_in),
            (w_down_hbm, w_down),
            (b_down_hbm, b_down),
            (g_down_hbm, g_down),
            (w_head_hbm, w_head),
            (b_head_hbm, b_head),
        )
    ):
        fetches[n] = pltpu.make_async_copy(source, target, arrived.at[n])
        fetches[n].start()
    me = lax.axis_index("wide")
    read_rows = frames.shape[0]
    clips = len_s.shape[0]
    rows = latents.shape[0]

    len0 = jnp.int32(0)
    len1 = jnp.int32(0)
    for c in range(clips):
        mine = reader_s[c] == me
        length = len_s[c]
        len1 = jnp.where(mine & (len0 > 0), length, len1)
        len0 = jnp.where(mine & (len0 == 0), length, len0)
    frames0 = 4 * len0 - 3


    order = arrangement(
        512,
        lambda i: ((i & 32) << 3) | ((i & 1) << 7) | ((i & 448) >> 2) | ((i & 30) >> 1),
    )
    for n in range(13):
        fetches[n].wait()
    split = []
    for h in range(2):
        piece = jnp.concatenate(
            [frames[:, k * 1024 + h * 512 : k * 1024 + (h + 1) * 512] for k in range(3)], axis=0
        )
        split.append(dot(piece, order))
    lane = iota((read_rows, 128), 1)
    across = lane & 15
    inside = {-1: across > 0, 1: across < 15}
    split = [part.astype(BF16) for part in split]
    zero = jnp.zeros((), BF16)
    for k in range(3):
        for r in range(4):
            for s in range(4):
                p = ((r + 1) % 2) * 2 + (s + 1) % 2
                low, high = (
                    part[k * read_rows : (k + 1) * read_rows, p * 128 : (p + 1) * 128]
                    for part in split
                )
                dy, dx = (-1, 0, 0, 1)[r], (-1, 0, 0, 1)[s]
                shift = -(dy * 16 + dx) % 128
                if shift:
                    low, high = pltpu.roll(low, shift, 1), pltpu.roll(high, shift, 1)
                if dy < 0:
                    low, high = jnp.where(lane < 16, zero, low), jnp.where(lane < 16, low, high)
                if dy > 0:
                    low, high = jnp.where(lane < 112, low, high), jnp.where(lane < 112, high, zero)
                if dx:
                    low, high = jnp.where(inside[dx], low, zero), jnp.where(inside[dx], high, zero)
                at = (k * 16 + r * 4 + s) * (read_rows + 1)
                raw[0, at : at + read_rows, :] = low.astype(F32)
                raw[1, at : at + read_rows, :] = high.astype(F32)

    def place(frame, carry):
        slot = frame + 2 + jnp.where(frame >= frames0, 2, 0)
        to = pl.multiple_of(slot * TAP, TAP)
        for h in range(2):
            patches[pl.ds(to, TAP), h * 128 : (h + 1) * 128] = raw[
                h, pl.ds(frame, TAP, stride=read_rows + 1), :
            ].astype(BF16)
        return carry

    for frame in range(read_rows):
        place(frame, 0)
    pick[...] = pick_rows(
        me, steps, rows, pick.shape[0], len_row[...], reader_row[...], owner_row[...]
    )

    gain_in[...] = jnp.broadcast_to(column(g_in[...]) * 0.5, gain_in.shape)
    gain_down[...] = jnp.broadcast_to(column(g_down[...]) * 0.5, gain_down.shape)
    bias_down[...] = jnp.broadcast_to(column(b_down[...]), bias_down.shape)
    bias = column(b_in[...])
    bias_high = bias.astype(BF16).astype(F32)
    bias_mid = (bias - bias_high).astype(BF16).astype(F32)
    bias_low = bias - bias_high - bias_mid
    lane = iota((128, DEPTH), 1)
    bias_lanes = jnp.where(
        lane == 144,
        bias_high,
        jnp.where(lane == 145, bias_mid, jnp.where(lane == 146, bias_low, 0.0)),
    )
    for p in range(4):
        taps = lax.dot_general(
            w_in[...], spread[p], (((0,), (0,)), ((), ())), preferred_element_type=F32
        )
        wide_in[p * 128 : (p + 1) * 128, :] = (taps + bias_lanes).astype(BF16)
    order = arrangement(512, lambda i: ((i & 3) << 7) | (i >> 2))
    wide_down[...] = dot(w_down[...], order).astype(BF16)
    order = arrangement(256, lambda i: ((i & 15) << 4) | (i >> 4))
    chunks = []
    for chunk in range(8):
        piece = jnp.concatenate(
            [w_head[:, s * 2048 + chunk * 256 : s * 2048 + (chunk + 1) * 256] for s in range(4)],
            axis=0,
        )
        chunks.append(dot(piece, order).astype(BF16))
    group = iota((64, 128), 1) >> 4
    for half in range(2):
        parts = [chunk[:, half * 128 : (half + 1) * 128] for chunk in chunks]
        for bit in (1, 2, 4):
            upper = (group & bit) != 0
            for i in range(8):
                if i & bit:
                    continue
                low, high = parts[i], parts[i | bit]
                parts[i] = jnp.where(upper, pltpu.roll(high, bit * 16, 1), low)
                parts[i | bit] = jnp.where(upper, high, pltpu.roll(low, 128 - bit * 16, 1))
        for i in range(8):
            at = (half * 8 + i) * 16
            for s in range(4):
                wide_head[at : at + 16, s * 128 : (s + 1) * 128] = parts[i][
                    s * 16 : (s + 1) * 16
                ]

    blank = jnp.zeros((2 * TAP, 256), BF16)
    patches[: 2 * TAP, :] = blank
    patches[pl.ds(pl.multiple_of((frames0 + 2) * TAP, TAP), 2 * TAP), :] = blank

    square = iota((1, 256), 1)
    corner = ((square >> 4 & 3) << 2) | (square & 3)
    ones = jnp.ones((16, 256), BF16)

    def convolve(columns):
        product = dot(wide_in[...], columns)
        return jnp.concatenate(
            [
                half_silu_norm(product[p * 128 : (p + 1) * 128], twice(gain_in[...]), False)
                for p in range(4)
            ],
            axis=0,
        )

    def lower(columns):
        return half_silu_norm(
            dot(wide_down[...], columns) + twice(bias_down[...]), twice(gain_down[...]), False
        )

    def keep(row, product):
        total = jnp.zeros((16, 256), F32)
        for ab in range(16):
            total = total + jnp.where(corner == ab, product[ab * 16 : (ab + 1) * 16], 0.0)
        partial[pl.ds(pl.multiple_of(row * 16, 16), 16), :] = total

    partial[...] = jnp.zeros_like(partial)

    def opening(base):
        taps = patches[pl.ds(pl.multiple_of(base * TAP, TAP), 3 * TAP), :]
        columns = jnp.concatenate([taps, ones], axis=0)
        return dot(wide_head[:, 384:], lower(convolve(columns)))

    count = len0 + len1 - 2

    def columns_of(frame):
        taps = patches[pl.ds(pl.multiple_of(frame * TAP, TAP), 3 * TAP), :]
        return jnp.concatenate([taps, ones], axis=0)

    def first_frame(i):
        second = i >= len0 - 1
        j = i + 1 - jnp.where(second, len0 - 1, 0)
        return 4 * j - 3 + jnp.where(second, frames0 + 2, 0)

    def first_half(i):
        first = first_frame(i)
        for s in range(4):
            merged[s] = convolve(columns_of(first + s))

    def second_half(i):
        row = jnp.where(count > 0, i + 1 + jnp.where(i >= len0 - 1, 1, 0), rows)
        reduced = jnp.concatenate([lower(merged[s]) for s in range(4)], axis=0)
        keep(row, dot(wide_head[...], reduced))

    keep(0, opening(0))
    first_half(0)

    def both(i, carry):
        row = i + 1 + jnp.where(i >= len0 - 1, 1, 0)
        first = first_frame(i + 1)
        reduced = []
        for s in range(4):
            reduced.append(lower(merged[s]))
            merged[s] = convolve(columns_of(first + s))
        keep(row, dot(wide_head[...], jnp.concatenate(reduced, axis=0)))
        return carry

    lax.fori_loop(0, count - 1, both, 0)

    second_half(count - 1)
    keep(len0, opening(frames0 + 2))

    place_of = iota((256, 128), 0)
    cell = ((place_of >> 6) << 2) | ((place_of & 15) >> 2)
    sums = one_hot(cell == (iota((256, 128), 1) & 15))
    sums = jnp.concatenate([sums, sums], axis=1)
    sums_of = partial[: rows * 16, :]
    high = sums_of.astype(BF16)
    spots = dot(high, sums) + dot((sums_of - high.astype(F32)).astype(BF16), sums)
    channel = (iota((16, 256), 1) >> 4) == iota((16, 256), 0)
    bias = jnp.sum(jnp.where(channel, column(b_head[...]), 0.0), axis=0, keepdims=True)
    spots = jnp.where(channel[None], spots.reshape(rows, 16, 256), 0.0)
    latents[...] = (jnp.sum(spots, axis=1) + bias).astype(BF16)


def encode(steps, own_rows, rows, frames, latent_len, reader, owner, weights):
    w_in, b_in, g_in, w_down, b_down, g_down, w_head, b_head = weights
    read_rows = frames.shape[0]
    vmem = pl.BlockSpec(memory_space=pltpu.VMEM)
    smem = pl.BlockSpec(memory_space=pltpu.SMEM)
    row = lambda x: x.reshape(1, -1)
    arrays = [
        frames,
        row(latent_len),
        row(reader),
        row(owner),
        patch_spread(),
        w_in.T,
        row(b_in),
        row(g_in),
        w_down,
        row(b_down),
        row(g_down),
        w_head,
        row(b_head),
    ]
    return pl.pallas_call(
        functools.partial(encode_kernel, steps),
        out_shape=(
            jax.ShapeDtypeStruct((rows, 256), BF16),
            jax.ShapeDtypeStruct((own_rows, rows << len(steps)), BF16),
        ),
        in_specs=[smem, smem] + [pl.BlockSpec(memory_space=pl.ANY)] * 13,
        out_specs=(vmem, vmem),
        scratch_shapes=[
            pltpu.VMEM((2, (read_rows + 1) * TAP, 128), F32),
            pltpu.VMEM(((read_rows + 4) * TAP, 256), BF16),
            pltpu.VMEM((512, DEPTH), BF16),
            pltpu.VMEM((128, 512), BF16),
            pltpu.VMEM((256, 512), BF16),
            pltpu.VMEM((128, 128), F32),
            pltpu.VMEM((128, 128), F32),
            pltpu.VMEM((128, 128), F32),
            pltpu.VMEM((rows * 16 + 16, 256), F32),
            pltpu.VMEM((4, 512, 256), BF16),
        ]
        + [pltpu.VMEM(x.shape, x.dtype) for x in arrays]
        + [pltpu.SemaphoreType.DMA((13,))],
    )(latent_len, reader, *arrays)


def shards(
    frames, latent_len, reader, owner, w_in, b_in, g_in, w_down, b_down, g_down, w_head, b_head
):
    weights = (w_in, b_in, g_in, w_down, b_down, g_down, w_head, b_head)
    wide_n = lax.axis_size("wide")
    steps = []
    step = wide_n // 2
    while step:
        steps.append(step)
        step //= 2
    most_read = frames.shape[0] // 4
    own_rows = 2 * ((most_read + 2) // 2)
    rows = -(-most_read // 16) * 16
    latents, pick = encode(steps, own_rows, rows, frames, latent_len, reader, owner, weights)
    for step in steps:
        pairs = [(i, i ^ step) for i in range(wide_n)]
        latents = jnp.concatenate([latents, lax.ppermute(latents, "wide", pairs)], axis=0)
    return jnp.dot(pick, latents, preferred_element_type=F32).astype(BF16)


def solution(mesh):
    return jax.shard_map(
        shards,
        mesh=mesh,
        in_specs=(P(("groups", "wide"), None), P("groups"), P("groups"), P("groups")) + (P(),) * 8,
        out_specs=P(("groups", "wide"), None),
        check_vma=False,
    )
```

```python
import functools

import jax
import jax.numpy as jnp
import numpy as np
from jax import lax
from jax.experimental import pallas as pl
from jax.experimental.pallas import tpu as pltpu
from jax.sharding import PartitionSpec as P

PIX = 32
EPS = 1e-06
TAP = 48
DEPTH = 160
F32 = jnp.float32
BF16 = jnp.bfloat16


def patch_spread():
    spread = np.zeros((4, 81, DEPTH), np.float32)
    for a2 in range(2):
        for b2 in range(2):
            for t in range(3):
                for a in range(3):
                    for b in range(3):
                        for k in range(3):
                            row = t * 27 + (a * 3 + b) * 3 + k
                            col = t * TAP + k * 16 + (a2 + a) * 4 + b2 + b
                            spread[2 * a2 + b2, row, col] = 1
    return jnp.asarray(spread, BF16)


def iota(shape, axis):
    return lax.broadcasted_iota(jnp.int32, shape, axis)


def one_hot(flags):
    return jnp.where(flags, 1.0, 0.0).astype(BF16)


def dot(a, b):
    return jnp.dot(a, b, preferred_element_type=F32)


def twice(x):
    return jnp.concatenate([x, x], axis=1)


def arrangement(size, move):
    to = move(iota((size, 128), 0))
    lane = iota((size, 128), 1)
    return jnp.concatenate([one_hot(to == lane + at) for at in range(0, size, 128)], axis=1)


def column(row):
    n = row.shape[1]
    eye = iota((n, n), 0) == iota((n, n), 1)
    return jnp.sum(jnp.where(eye, row, 0.0), axis=1, keepdims=True)


def half_silu_norm(values, half_gain, narrow):
    mean_square = jnp.sum(values * values, axis=0, keepdims=True) * (1.0 / values.shape[0])
    h = values * lax.rsqrt(mean_square + EPS) * half_gain
    if narrow:
        h = h.astype(BF16)
    return (h + h * jnp.tanh(h)).astype(BF16)


def pick_rows(me, steps, rows, own_rows, len_row, reader_row, owner_row):
    clips = len_row.shape[1]
    lens = len_row.astype(F32)
    len_col = column(lens)
    reader_col = column(reader_row.astype(F32))
    owner_col = column(owner_row.astype(F32))
    earlier = iota((clips, clips), 0) < iota((clips, clips), 1)
    same_reader = reader_col == reader_row.astype(F32)
    same_owner = owner_col == owner_row.astype(F32)
    read_off = jnp.sum(jnp.where(earlier & same_reader, len_col, 0.0), axis=0, keepdims=True)
    own_off = jnp.sum(jnp.where(earlier & same_owner, len_col, 0.0), axis=0, keepdims=True)
    away = reader_row ^ me
    block = jnp.zeros_like(away)
    core = away & 1
    for at, step in enumerate(steps[:-1]):
        across = jnp.where((away & (step - 1)) != 0, 1, 0)
        core = core ^ across
        block = block | (across << at)
    block = block | (core << (len(steps) - 1))
    slot = iota((own_rows, clips), 0).astype(F32)
    inside = (owner_row == me) & (own_off <= slot) & (slot < own_off + lens)
    source = block.astype(F32) * rows + read_off - own_off + slot
    source = jnp.sum(jnp.where(inside, source + 1.0, 0.0), axis=1, keepdims=True) - 1.0
    width = rows << len(steps)
    return one_hot(iota((own_rows, width), 1).astype(F32) == source)


def encode_kernel(
    steps,
    frames_hbm,
    len_row_hbm,
    reader_row_hbm,
    owner_row_hbm,
    spread_hbm,
    w_in_hbm,
    b_in_hbm,
    g_in_hbm,
    w_down_hbm,
    b_down_hbm,
    g_down_hbm,
    w_head_hbm,
    b_head_hbm,
    latents,
    pick_hbm,
    raw,
    patches,
    wide_in,
    wide_down,
    wide_head,
    gain_in,
    gain_down,
    bias_down,
    partial,
    merged,
    frames,
    len_row,
    reader_row,
    owner_row,
    spread,
    w_in,
    b_in,
    g_in,
    w_down,
    b_down,
    g_down,
    w_head,
    b_head,
    len_s,
    reader_s,
    pick,
    arrived,
):
    fetches = {}
    for n, (source, target) in enumerate(
        (
            (frames_hbm, frames),
            (len_row_hbm, len_row),
            (reader_row_hbm, reader_row),
            (owner_row_hbm, owner_row),
            (spread_hbm, spread),
            (w_in_hbm, w_in),
            (b_in_hbm, b_in),
            (g_in_hbm, g_in),
            (w_down_hbm, w_down),
            (b_down_hbm, b_down),
            (g_down_hbm, g_down),
            (w_head_hbm, w_head),
            (b_head_hbm, b_head),
            (len_row_hbm, len_s),
            (reader_row_hbm, reader_s),
        )
    ):
        fetches[n] = pltpu.make_async_copy(source, target, arrived.at[n])
        fetches[n].start()
    me = lax.axis_index("wide")
    read_rows = frames.shape[0]
    clips = len_s.shape[1]
    rows = latents.shape[0]

    order = arrangement(
        512,
        lambda i: ((i & 32) << 3) | ((i & 1) << 7) | ((i & 448) >> 2) | ((i & 30) >> 1),
    )
    for n in range(15):
        fetches[n].wait()

    len0 = jnp.int32(0)
    len1 = jnp.int32(0)
    for c in range(clips):
        mine = reader_s[0, c] == me
        length = len_s[0, c]
        len1 = jnp.where(mine & (len0 > 0), length, len1)
        len0 = jnp.where(mine & (len0 == 0), length, len0)
    frames0 = 4 * len0 - 3

    split = []
    for h in range(2):
        piece = jnp.concatenate(
            [frames[:, k * 1024 + h * 512 : k * 1024 + (h + 1) * 512] for k in range(3)], axis=0
        )
        split.append(dot(piece, order))
    lane = iota((read_rows, 128), 1)
    across = lane & 15
    inside = {-1: across > 0, 1: across < 15}
    split = [part.astype(BF16) for part in split]
    zero = jnp.zeros((), BF16)
    for k in range(3):
        for r in range(4):
            for s in range(4):
                p = ((r + 1) % 2) * 2 + (s + 1) % 2
                low, high = (
                    part[k * read_rows : (k + 1) * read_rows, p * 128 : (p + 1) * 128]
                    for part in split
                )
                dy, dx = (-1, 0, 0, 1)[r], (-1, 0, 0, 1)[s]
                shift = -(dy * 16 + dx) % 128
                if shift:
                    low, high = pltpu.roll(low, shift, 1), pltpu.roll(high, shift, 1)
                if dy < 0:
                    low, high = jnp.where(lane < 16, zero, low), jnp.where(lane < 16, low, high)
                if dy > 0:
                    low, high = jnp.where(lane < 112, low, high), jnp.where(lane < 112, high, zero)
                if dx:
                    low, high = jnp.where(inside[dx], low, zero), jnp.where(inside[dx], high, zero)
                at = (k * 16 + r * 4 + s) * (read_rows + 1)
                raw[0, at : at + read_rows, :] = low.astype(F32)
                raw[1, at : at + read_rows, :] = high.astype(F32)

    def place(frame, carry):
        slot = frame + 2 + jnp.where(frame >= frames0, 2, 0)
        to = pl.multiple_of(slot * TAP, TAP)
        for h in range(2):
            patches[pl.ds(to, TAP), h * 128 : (h + 1) * 128] = raw[
                h, pl.ds(frame, TAP, stride=read_rows + 1), :
            ].astype(BF16)
        return carry

    for frame in range(read_rows):
        place(frame, 0)
    pick[...] = pick_rows(
        me, steps, rows, pick.shape[0], len_row[...], reader_row[...], owner_row[...]
    )
    picked = pltpu.make_async_copy(pick, pick_hbm, arrived.at[15])
    picked.start()

    gain_in[...] = jnp.broadcast_to(column(g_in[...]) * 0.5, gain_in.shape)
    gain_down[...] = jnp.broadcast_to(column(g_down[...]) * 0.5, gain_down.shape)
    bias_down[...] = jnp.broadcast_to(column(b_down[...]), bias_down.shape)
    bias = column(b_in[...])
    bias_high = bias.astype(BF16).astype(F32)
    bias_mid = (bias - bias_high).astype(BF16).astype(F32)
    bias_low = bias - bias_high - bias_mid
    lane = iota((128, DEPTH), 1)
    bias_lanes = jnp.where(
        lane == 144,
        bias_high,
        jnp.where(lane == 145, bias_mid, jnp.where(lane == 146, bias_low, 0.0)),
    )
    for p in range(4):
        taps = lax.dot_general(
            w_in[...], spread[p], (((0,), (0,)), ((), ())), preferred_element_type=F32
        )
        wide_in[p * 128 : (p + 1) * 128, :] = (taps + bias_lanes).astype(BF16)
    order = arrangement(512, lambda i: ((i & 3) << 7) | (i >> 2))
    wide_down[...] = dot(w_down[...], order).astype(BF16)
    order = arrangement(256, lambda i: ((i & 15) << 4) | (i >> 4))
    chunks = []
    for chunk in range(8):
        piece = jnp.concatenate(
            [w_head[:, s * 2048 + chunk * 256 : s * 2048 + (chunk + 1) * 256] for s in range(4)],
            axis=0,
        )
        chunks.append(dot(piece, order).astype(BF16))
    group = iota((64, 128), 1) >> 4
    for half in range(2):
        parts = [chunk[:, half * 128 : (half + 1) * 128] for chunk in chunks]
        for bit in (1, 2, 4):
            upper = (group & bit) != 0
            for i in range(8):
                if i & bit:
                    continue
                low, high = parts[i], parts[i | bit]
                parts[i] = jnp.where(upper, pltpu.roll(high, bit * 16, 1), low)
                parts[i | bit] = jnp.where(upper, high, pltpu.roll(low, 128 - bit * 16, 1))
        for i in range(8):
            at = (half * 8 + i) * 16
            for s in range(4):
                wide_head[at : at + 16, s * 128 : (s + 1) * 128] = parts[i][
                    s * 16 : (s + 1) * 16
                ]

    blank = jnp.zeros((2 * TAP, 256), BF16)
    patches[: 2 * TAP, :] = blank
    patches[pl.ds(pl.multiple_of((frames0 + 2) * TAP, TAP), 2 * TAP), :] = blank

    square = iota((1, 256), 1)
    corner = ((square >> 4 & 3) << 2) | (square & 3)
    ones = jnp.ones((16, 256), BF16)

    def convolve(columns):
        product = dot(wide_in[...], columns)
        return jnp.concatenate(
            [
                half_silu_norm(product[p * 128 : (p + 1) * 128], twice(gain_in[...]), False)
                for p in range(4)
            ],
            axis=0,
        )

    def lower(columns):
        return half_silu_norm(
            dot(wide_down[...], columns) + twice(bias_down[...]), twice(gain_down[...]), False
        )

    def keep(row, product):
        total = jnp.zeros((16, 256), F32)
        for ab in range(16):
            total = total + jnp.where(corner == ab, product[ab * 16 : (ab + 1) * 16], 0.0)
        partial[pl.ds(pl.multiple_of(row * 16, 16), 16), :] = total

    partial[...] = jnp.zeros_like(partial)

    def opening(base):
        taps = patches[pl.ds(pl.multiple_of(base * TAP, TAP), 3 * TAP), :]
        columns = jnp.concatenate([taps, ones], axis=0)
        return dot(wide_head[:, 384:], lower(convolve(columns)))

    count = len0 + len1 - 2

    def columns_of(frame):
        taps = patches[pl.ds(pl.multiple_of(frame * TAP, TAP), 3 * TAP), :]
        return jnp.concatenate([taps, ones], axis=0)

    def first_frame(i):
        second = i >= len0 - 1
        j = i + 1 - jnp.where(second, len0 - 1, 0)
        return 4 * j - 3 + jnp.where(second, frames0 + 2, 0)

    def first_half(i):
        first = first_frame(i)
        for s in range(4):
            merged[s] = convolve(columns_of(first + s))

    def second_half(i):
        row = jnp.where(count > 0, i + 1 + jnp.where(i >= len0 - 1, 1, 0), rows)
        reduced = jnp.concatenate([lower(merged[s]) for s in range(4)], axis=0)
        keep(row, dot(wide_head[...], reduced))

    keep(0, opening(0))
    first_half(0)

    def both(i, carry):
        row = i + 1 + jnp.where(i >= len0 - 1, 1, 0)
        first = first_frame(i + 1)
        reduced = []
        for s in range(4):
            reduced.append(lower(merged[s]))
            merged[s] = convolve(columns_of(first + s))
        keep(row, dot(wide_head[...], jnp.concatenate(reduced, axis=0)))
        return carry

    lax.fori_loop(0, count - 1, both, 0)

    second_half(count - 1)
    keep(len0, opening(frames0 + 2))

    place_of = iota((256, 128), 0)
    cell = ((place_of >> 6) << 2) | ((place_of & 15) >> 2)
    sums = one_hot(cell == (iota((256, 128), 1) & 15))
    sums = jnp.concatenate([sums, sums], axis=1)
    sums_of = partial[: rows * 16, :]
    high = sums_of.astype(BF16)
    spots = dot(high, sums) + dot((sums_of - high.astype(F32)).astype(BF16), sums)
    channel = (iota((16, 256), 1) >> 4) == iota((16, 256), 0)
    bias = jnp.sum(jnp.where(channel, column(b_head[...]), 0.0), axis=0, keepdims=True)
    spots = jnp.where(channel[None], spots.reshape(rows, 16, 256), 0.0)
    latents[...] = (jnp.sum(spots, axis=1) + bias).astype(BF16)
    picked.wait()


def encode(steps, own_rows, rows, frames, latent_len, reader, owner, weights):
    w_in, b_in, g_in, w_down, b_down, g_down, w_head, b_head = weights
    read_rows = frames.shape[0]
    vmem = pl.BlockSpec(memory_space=pltpu.VMEM)
    row = lambda x: x.reshape(1, -1)
    arrays = [
        frames,
        row(latent_len),
        row(reader),
        row(owner),
        patch_spread(),
        w_in.T,
        row(b_in),
        row(g_in),
        w_down,
        row(b_down),
        row(g_down),
        w_head,
        row(b_head),
    ]
    return pl.pallas_call(
        functools.partial(encode_kernel, steps),
        out_shape=(
            jax.ShapeDtypeStruct((rows, 256), BF16),
            jax.ShapeDtypeStruct((own_rows, rows << len(steps)), BF16),
        ),
        in_specs=[pl.BlockSpec(memory_space=pl.ANY)] * 13,
        out_specs=(vmem, pl.BlockSpec(memory_space=pl.ANY)),
        scratch_shapes=[
            pltpu.VMEM((2, (read_rows + 1) * TAP, 128), F32),
            pltpu.VMEM(((read_rows + 4) * TAP, 256), BF16),
            pltpu.VMEM((512, DEPTH), BF16),
            pltpu.VMEM((128, 512), BF16),
            pltpu.VMEM((256, 512), BF16),
            pltpu.VMEM((128, 128), F32),
            pltpu.VMEM((128, 128), F32),
            pltpu.VMEM((128, 128), F32),
            pltpu.VMEM((rows * 16 + 16, 256), F32),
            pltpu.VMEM((4, 512, 256), BF16),
        ]
        + [pltpu.VMEM(x.shape, x.dtype) for x in arrays]
        + [pltpu.SMEM((1, latent_len.shape[0]), jnp.int32)] * 2
        + [
            pltpu.VMEM((own_rows, rows << len(steps)), BF16),
            pltpu.SemaphoreType.DMA((16,)),
        ],
    )(*arrays)


def shards(
    frames, latent_len, reader, owner, w_in, b_in, g_in, w_down, b_down, g_down, w_head, b_head
):
    weights = (w_in, b_in, g_in, w_down, b_down, g_down, w_head, b_head)
    wide_n = lax.axis_size("wide")
    steps = []
    step = wide_n // 2
    while step > 1:
        steps.append(step + 1)
        step //= 2
    steps.append(1)
    most_read = frames.shape[0] // 4
    own_rows = 2 * ((most_read + 2) // 2)
    rows = -(-most_read // 16) * 16
    latents, pick = encode(steps, own_rows, rows, frames, latent_len, reader, owner, weights)
    for step in steps:
        pairs = [(i, i ^ step) for i in range(wide_n)]
        latents = jnp.concatenate([latents, lax.ppermute(latents, "wide", pairs)], axis=0)
    return jnp.dot(pick, latents, preferred_element_type=F32).astype(BF16)


def solution(mesh):
    return jax.shard_map(
        shards,
        mesh=mesh,
        in_specs=(P(("groups", "wide"), None), P("groups"), P("groups"), P("groups")) + (P(),) * 8,
        out_specs=P(("groups", "wide"), None),
        check_vma=False,
    )
```

```python
import functools

import jax
import jax.numpy as jnp
import numpy as np
from jax import lax
from jax.experimental import pallas as pl
from jax.experimental.pallas import tpu as pltpu
from jax.sharding import PartitionSpec as P

PIX = 32
EPS = 1e-06
TAP = 48
DEPTH = 160
F32 = jnp.float32
BF16 = jnp.bfloat16


def patch_spread():
    spread = np.zeros((4, 81, DEPTH), np.float32)
    for a2 in range(2):
        for b2 in range(2):
            for t in range(3):
                for a in range(3):
                    for b in range(3):
                        for k in range(3):
                            row = t * 27 + (a * 3 + b) * 3 + k
                            col = t * TAP + k * 16 + (a2 + a) * 4 + b2 + b
                            spread[2 * a2 + b2, row, col] = 1
    return jnp.asarray(spread, BF16)


def iota(shape, axis):
    return lax.broadcasted_iota(jnp.int32, shape, axis)


def one_hot(flags):
    return jnp.where(flags, 1.0, 0.0).astype(BF16)


def dot(a, b):
    return jnp.dot(a, b, preferred_element_type=F32)


def twice(x):
    return jnp.concatenate([x, x], axis=1)


def arrangement(size, move):
    to = move(iota((size, 128), 0))
    lane = iota((size, 128), 1)
    return jnp.concatenate([one_hot(to == lane + at) for at in range(0, size, 128)], axis=1)


def column(row):
    n = row.shape[1]
    eye = iota((n, n), 0) == iota((n, n), 1)
    return jnp.sum(jnp.where(eye, row, 0.0), axis=1, keepdims=True)


def half_silu_norm(values, half_gain, narrow):
    mean_square = jnp.sum(values * values, axis=0, keepdims=True) * (1.0 / values.shape[0])
    h = values * lax.rsqrt(mean_square + EPS) * half_gain
    if narrow:
        h = h.astype(BF16)
    return (h + h * jnp.tanh(h)).astype(BF16)


def pick_rows(me, steps, rows, own_rows, len_row, reader_row, owner_row):
    clips = len_row.shape[1]
    lens = len_row.astype(F32)
    len_col = column(lens)
    reader_col = column(reader_row.astype(F32))
    owner_col = column(owner_row.astype(F32))
    earlier = iota((clips, clips), 0) < iota((clips, clips), 1)
    same_reader = reader_col == reader_row.astype(F32)
    same_owner = owner_col == owner_row.astype(F32)
    read_off = jnp.sum(jnp.where(earlier & same_reader, len_col, 0.0), axis=0, keepdims=True)
    own_off = jnp.sum(jnp.where(earlier & same_owner, len_col, 0.0), axis=0, keepdims=True)
    away = reader_row ^ me
    block = jnp.zeros_like(away)
    core = away & 1
    for at, step in enumerate(steps[:-1]):
        across = jnp.where((away & (step - 1)) != 0, 1, 0)
        core = core ^ across
        block = block | (across << at)
    block = block | (core << (len(steps) - 1))
    slot = iota((own_rows, clips), 0).astype(F32)
    inside = (owner_row == me) & (own_off <= slot) & (slot < own_off + lens)
    source = block.astype(F32) * rows + read_off - own_off + slot
    source = jnp.sum(jnp.where(inside, source + 1.0, 0.0), axis=1, keepdims=True) - 1.0
    width = rows << len(steps)
    return one_hot(iota((own_rows, width), 1).astype(F32) == source)


BLOCK = 4


def encode_kernel(
    steps,
    frames_hbm,
    len_row_hbm,
    reader_row_hbm,
    owner_row_hbm,
    spread_hbm,
    w_in_hbm,
    b_in_hbm,
    g_in_hbm,
    w_down_hbm,
    b_down_hbm,
    g_down_hbm,
    w_head_hbm,
    b_head_hbm,
    latents,
    pick_hbm,
    raw,
    patches,
    wide_in,
    wide_down,
    wide_head,
    gain_in,
    gain_down,
    bias_down,
    partial,
    merged,
    frames,
    len_row,
    reader_row,
    owner_row,
    spread,
    w_in,
    b_in,
    g_in,
    w_down,
    b_down,
    g_down,
    w_head,
    b_head,
    len_s,
    reader_s,
    pick,
    arrived,
):
    fetches = {}
    for n, (source, target) in enumerate(
        (
            (frames_hbm, frames),
            (len_row_hbm, len_row),
            (reader_row_hbm, reader_row),
            (owner_row_hbm, owner_row),
            (spread_hbm, spread),
            (w_in_hbm, w_in),
            (b_in_hbm, b_in),
            (g_in_hbm, g_in),
            (w_down_hbm, w_down),
            (b_down_hbm, b_down),
            (g_down_hbm, g_down),
            (w_head_hbm, w_head),
            (b_head_hbm, b_head),
            (len_row_hbm, len_s),
            (reader_row_hbm, reader_s),
        )
    ):
        fetches[n] = pltpu.make_async_copy(source, target, arrived.at[n])
        fetches[n].start()
    me = lax.axis_index("wide")
    read_rows = frames.shape[0]
    clips = len_s.shape[1]
    rows = latents.shape[0]

    order = arrangement(
        512,
        lambda i: ((i & 32) << 3) | ((i & 1) << 7) | ((i & 448) >> 2) | ((i & 30) >> 1),
    )
    for n in range(15):
        fetches[n].wait()

    len0 = jnp.int32(0)
    len1 = jnp.int32(0)
    for c in range(clips):
        mine = reader_s[0, c] == me
        length = len_s[0, c]
        len1 = jnp.where(mine & (len0 > 0), length, len1)
        len0 = jnp.where(mine & (len0 == 0), length, len0)
    frames0 = 4 * len0 - 3

    split = []
    for h in range(2):
        piece = jnp.concatenate(
            [frames[:, k * 1024 + h * 512 : k * 1024 + (h + 1) * 512] for k in range(3)], axis=0
        )
        split.append(dot(piece, order))
    lane = iota((read_rows, 128), 1)
    across = lane & 15
    inside = {-1: across > 0, 1: across < 15}
    split = [part.astype(BF16) for part in split]
    zero = jnp.zeros((), BF16)
    for k in range(3):
        for r in range(4):
            for s in range(4):
                p = ((r + 1) % 2) * 2 + (s + 1) % 2
                low, high = (
                    part[k * read_rows : (k + 1) * read_rows, p * 128 : (p + 1) * 128]
                    for part in split
                )
                dy, dx = (-1, 0, 0, 1)[r], (-1, 0, 0, 1)[s]
                shift = -(dy * 16 + dx) % 128
                if shift:
                    low, high = pltpu.roll(low, shift, 1), pltpu.roll(high, shift, 1)
                if dy < 0:
                    low, high = jnp.where(lane < 16, zero, low), jnp.where(lane < 16, low, high)
                if dy > 0:
                    low, high = jnp.where(lane < 112, low, high), jnp.where(lane < 112, high, zero)
                if dx:
                    low, high = jnp.where(inside[dx], low, zero), jnp.where(inside[dx], high, zero)
                at = (k * 16 + r * 4 + s) * (read_rows + 1)
                raw[0, at : at + read_rows, :] = low.astype(F32)
                raw[1, at : at + read_rows, :] = high.astype(F32)

    def place(frame, carry):
        slot = frame + 2 + jnp.where(frame >= frames0, 2, 0)
        to = pl.multiple_of(slot * TAP, TAP)
        for h in range(2):
            patches[h, pl.ds(to, TAP), :] = raw[
                h, pl.ds(frame, TAP, stride=read_rows + 1), :
            ].astype(BF16)
        return carry

    for frame in range(read_rows):
        place(frame, 0)
    pick[...] = pick_rows(
        me, steps, rows, pick.shape[0], len_row[...], reader_row[...], owner_row[...]
    )
    picked = pltpu.make_async_copy(pick, pick_hbm, arrived.at[15])
    picked.start()

    gain_in[...] = jnp.broadcast_to(column(g_in[...]) * 0.5, gain_in.shape)
    gain_down[...] = jnp.broadcast_to(column(g_down[...]) * 0.5, gain_down.shape)
    bias_down[...] = jnp.broadcast_to(column(b_down[...]), bias_down.shape)
    bias = column(b_in[...])
    bias_high = bias.astype(BF16).astype(F32)
    bias_mid = (bias - bias_high).astype(BF16).astype(F32)
    bias_low = bias - bias_high - bias_mid
    lane = iota((128, DEPTH), 1)
    bias_lanes = jnp.where(
        lane == 144,
        bias_high,
        jnp.where(lane == 145, bias_mid, jnp.where(lane == 146, bias_low, 0.0)),
    )
    for p in range(4):
        taps = lax.dot_general(
            w_in[...], spread[p], (((0,), (0,)), ((), ())), preferred_element_type=F32
        )
        wide_in[p * 128 : (p + 1) * 128, :] = (taps + bias_lanes).astype(BF16)
    order = arrangement(512, lambda i: ((i & 3) << 7) | (i >> 2))
    wide_down[...] = dot(w_down[...], order).astype(BF16)
    order = arrangement(256, lambda i: ((i & 15) << 4) | (i >> 4))
    chunks = []
    for chunk in range(8):
        piece = jnp.concatenate(
            [w_head[:, s * 2048 + chunk * 256 : s * 2048 + (chunk + 1) * 256] for s in range(4)],
            axis=0,
        )
        chunks.append(dot(piece, order).astype(BF16))
    group = iota((64, 128), 1) >> 4
    for half in range(2):
        parts = [chunk[:, half * 128 : (half + 1) * 128] for chunk in chunks]
        for bit in (1, 2, 4):
            upper = (group & bit) != 0
            for i in range(8):
                if i & bit:
                    continue
                low, high = parts[i], parts[i | bit]
                parts[i] = jnp.where(upper, pltpu.roll(high, bit * 16, 1), low)
                parts[i | bit] = jnp.where(upper, high, pltpu.roll(low, 128 - bit * 16, 1))
        for i in range(8):
            at = (half * 8 + i) * 16
            for s in range(4):
                wide_head[at : at + 16, s * 128 : (s + 1) * 128] = parts[i][
                    s * 16 : (s + 1) * 16
                ]

    patches[:, : 2 * TAP, :] = jnp.zeros((2, 2 * TAP, 128), BF16)
    patches[:, pl.ds(pl.multiple_of((frames0 + 2) * TAP, TAP), 2 * TAP), :] = jnp.zeros(
        (2, 2 * TAP, 128), BF16
    )

    square = iota((1, 256), 1)
    corner = ((square >> 4 & 3) << 2) | (square & 3)
    ones = jnp.ones((16, 256), BF16)

    def columns_of(frame):
        at = pl.ds(pl.multiple_of(frame * TAP, TAP), 3 * TAP)
        taps = jnp.concatenate([patches[0, at, :], patches[1, at, :]], axis=1)
        return jnp.concatenate([taps, ones], axis=0)

    def convolve(columns):
        product = dot(wide_in[...], columns)
        return jnp.concatenate(
            [
                half_silu_norm(product[p * 128 : (p + 1) * 128], twice(gain_in[...]), False)
                for p in range(4)
            ],
            axis=0,
        )

    def lower(columns):
        return half_silu_norm(
            dot(wide_down[...], columns) + twice(bias_down[...]), twice(gain_down[...]), False
        )

    def keep(row, product):
        total = jnp.zeros((16, 256), F32)
        for ab in range(16):
            total = total + jnp.where(corner == ab, product[ab * 16 : (ab + 1) * 16], 0.0)
        partial[pl.ds(pl.multiple_of(row * 16, 16), 16), :] = total

    partial[...] = jnp.zeros_like(partial)

    def opening(base):
        columns = columns_of(base)
        return dot(wide_head[:, 384:], lower(convolve(columns)))

    count = len0 + len1 - 2

    def first_frame(i):
        second = i >= len0 - 1
        j = i + 1 - jnp.where(second, len0 - 1, 0)
        return 4 * j - 3 + jnp.where(second, frames0 + 2, 0)

    def first_half(i):
        first = first_frame(i)
        for s in range(4):
            full = convolve(columns_of(first + s))
            merged[s, 0], merged[s, 1] = full[:, :128], full[:, 128:]

    def held(s):
        return jnp.concatenate([merged[s, 0], merged[s, 1]], axis=1)

    def hold(s, full):
        merged[s, 0], merged[s, 1] = full[:, :128], full[:, 128:]

    def row_of(i):
        return jnp.where(count > 0, i + 1 + jnp.where(i >= len0 - 1, 1, 0), rows)

    def head(i, reduced):
        keep(row_of(i), dot(wide_head[...], jnp.concatenate(reduced, axis=0)))

    keep(0, opening(0))
    first_half(0)

    def turns(i, n):
        full = [held(s) for s in range(4)]
        for d in range(n):
            first = first_frame(i + d + 1)
            reduced, behind = [], []
            for s in range(4):
                reduced.append(lower(full[s]))
                behind.append(convolve(columns_of(first + s)))
                if d == n - 1:
                    hold(s, behind[s])
            head(i + d, reduced)
            full = behind

    blocks = jnp.maximum(count - 1, 0) // BLOCK

    def block(k, carry):
        turns(BLOCK * k, BLOCK)
        return carry

    def single(i, carry):
        turns(i, 1)
        return carry

    lax.fori_loop(0, blocks, block, 0)
    lax.fori_loop(BLOCK * blocks, count - 1, single, 0)
    head(count - 1, [lower(held(s)) for s in range(4)])
    keep(len0, opening(frames0 + 2))

    place_of = iota((256, 128), 0)
    cell = ((place_of >> 6) << 2) | ((place_of & 15) >> 2)
    sums = one_hot(cell == (iota((256, 128), 1) & 15))
    sums = jnp.concatenate([sums, sums], axis=1)
    sums_of = partial[: rows * 16, :]
    high = sums_of.astype(BF16)
    spots = dot(high, sums) + dot((sums_of - high.astype(F32)).astype(BF16), sums)
    channel = (iota((16, 256), 1) >> 4) == iota((16, 256), 0)
    bias = jnp.sum(jnp.where(channel, column(b_head[...]), 0.0), axis=0, keepdims=True)
    spots = jnp.where(channel[None], spots.reshape(rows, 16, 256), 0.0)
    latents[...] = (jnp.sum(spots, axis=1) + bias).astype(BF16)
    picked.wait()


def encode(steps, own_rows, rows, frames, latent_len, reader, owner, weights):
    w_in, b_in, g_in, w_down, b_down, g_down, w_head, b_head = weights
    read_rows = frames.shape[0]
    vmem = pl.BlockSpec(memory_space=pltpu.VMEM)
    row = lambda x: x.reshape(1, -1)
    arrays = [
        frames,
        row(latent_len),
        row(reader),
        row(owner),
        patch_spread(),
        w_in.T,
        row(b_in),
        row(g_in),
        w_down,
        row(b_down),
        row(g_down),
        w_head,
        row(b_head),
    ]
    return pl.pallas_call(
        functools.partial(encode_kernel, steps),
        out_shape=(
            jax.ShapeDtypeStruct((rows, 256), BF16),
            jax.ShapeDtypeStruct((own_rows, rows << len(steps)), BF16),
        ),
        in_specs=[pl.BlockSpec(memory_space=pl.ANY)] * 13,
        out_specs=(vmem, pl.BlockSpec(memory_space=pl.ANY)),
        scratch_shapes=[
            pltpu.VMEM((2, (read_rows + 1) * TAP, 128), F32),
            pltpu.VMEM((2, (read_rows + 4) * TAP, 128), BF16),
            pltpu.VMEM((512, DEPTH), BF16),
            pltpu.VMEM((128, 512), BF16),
            pltpu.VMEM((256, 512), BF16),
            pltpu.VMEM((128, 128), F32),
            pltpu.VMEM((128, 128), F32),
            pltpu.VMEM((128, 128), F32),
            pltpu.VMEM((rows * 16 + 16, 256), F32),
            pltpu.VMEM((4, 2, 512, 128), BF16),
        ]
        + [pltpu.VMEM(x.shape, x.dtype) for x in arrays]
        + [pltpu.SMEM((1, latent_len.shape[0]), jnp.int32)] * 2
        + [
            pltpu.VMEM((own_rows, rows << len(steps)), BF16),
            pltpu.SemaphoreType.DMA((16,)),
        ],
    )(*arrays)


def shards(
    frames, latent_len, reader, owner, w_in, b_in, g_in, w_down, b_down, g_down, w_head, b_head
):
    weights = (w_in, b_in, g_in, w_down, b_down, g_down, w_head, b_head)
    wide_n = lax.axis_size("wide")
    steps = []
    step = wide_n // 2
    while step > 1:
        steps.append(step + 1)
        step //= 2
    steps.append(1)
    most_read = frames.shape[0] // 4
    own_rows = 2 * ((most_read + 2) // 2)
    rows = -(-most_read // 16) * 16
    latents, pick = encode(steps, own_rows, rows, frames, latent_len, reader, owner, weights)
    for step in steps:
        pairs = [(i, i ^ step) for i in range(wide_n)]
        latents = jnp.concatenate([latents, lax.ppermute(latents, "wide", pairs)], axis=0)
    return jnp.dot(pick, latents, preferred_element_type=F32).astype(BF16)


def solution(mesh):
    return jax.shard_map(
        shards,
        mesh=mesh,
        in_specs=(P(("groups", "wide"), None), P("groups"), P("groups"), P("groups")) + (P(),) * 8,
        out_specs=P(("groups", "wide"), None),
        check_vma=False,
    )
```

```python
import functools

import jax
import jax.numpy as jnp
import numpy as np
from jax import lax
from jax.experimental import pallas as pl
from jax.experimental.pallas import tpu as pltpu
from jax.sharding import PartitionSpec as P

PIX = 32
EPS = 1e-06
TAP = 48
DEPTH = 160
F32 = jnp.float32
BF16 = jnp.bfloat16


def patch_spread():
    spread = np.zeros((4, 81, DEPTH), np.float32)
    for a2 in range(2):
        for b2 in range(2):
            for t in range(3):
                for a in range(3):
                    for b in range(3):
                        for k in range(3):
                            row = t * 27 + (a * 3 + b) * 3 + k
                            col = t * TAP + k * 16 + (a2 + a) * 4 + b2 + b
                            spread[2 * a2 + b2, row, col] = 1
    return jnp.asarray(spread, BF16)


def iota(shape, axis):
    return lax.broadcasted_iota(jnp.int32, shape, axis)


def one_hot(flags):
    return jnp.where(flags, 1.0, 0.0).astype(BF16)


def dot(a, b):
    return jnp.dot(a, b, preferred_element_type=F32)


def twice(x):
    return jnp.concatenate([x, x], axis=1)


def arrangement(size, move):
    to = move(iota((size, 128), 0))
    lane = iota((size, 128), 1)
    return jnp.concatenate([one_hot(to == lane + at) for at in range(0, size, 128)], axis=1)


def column(row):
    n = row.shape[1]
    eye = iota((n, n), 0) == iota((n, n), 1)
    return jnp.sum(jnp.where(eye, row, 0.0), axis=1, keepdims=True)


def half_silu_norm(values, half_gain, narrow):
    mean_square = jnp.sum(values * values, axis=0, keepdims=True) * (1.0 / values.shape[0])
    h = values * lax.rsqrt(mean_square + EPS) * half_gain
    if narrow:
        h = h.astype(BF16)
    return (h + h * jnp.tanh(h)).astype(BF16)


def pick_rows(me, steps, rows, own_rows, len_row, reader_row, owner_row):
    clips = len_row.shape[1]
    lens = len_row.astype(F32)
    len_col = column(lens)
    reader_col = column(reader_row.astype(F32))
    owner_col = column(owner_row.astype(F32))
    earlier = iota((clips, clips), 0) < iota((clips, clips), 1)
    same_reader = reader_col == reader_row.astype(F32)
    same_owner = owner_col == owner_row.astype(F32)
    read_off = jnp.sum(jnp.where(earlier & same_reader, len_col, 0.0), axis=0, keepdims=True)
    own_off = jnp.sum(jnp.where(earlier & same_owner, len_col, 0.0), axis=0, keepdims=True)
    away = reader_row ^ me
    block = jnp.zeros_like(away)
    core = away & 1
    for at, step in enumerate(steps[:-1]):
        across = jnp.where((away & (step - 1)) != 0, 1, 0)
        core = core ^ across
        block = block | (across << at)
    block = block | (core << (len(steps) - 1))
    slot = iota((own_rows, clips), 0).astype(F32)
    inside = (owner_row == me) & (own_off <= slot) & (slot < own_off + lens)
    source = block.astype(F32) * rows + read_off - own_off + slot
    source = jnp.sum(jnp.where(inside, source + 1.0, 0.0), axis=1, keepdims=True) - 1.0
    width = rows << len(steps)
    return one_hot(iota((own_rows, width), 1).astype(F32) == source)


BLOCK = 6


def encode_kernel(
    steps,
    frames_hbm,
    len_row_hbm,
    reader_row_hbm,
    owner_row_hbm,
    spread_hbm,
    w_in_hbm,
    b_in_hbm,
    g_in_hbm,
    w_down_hbm,
    b_down_hbm,
    g_down_hbm,
    w_head_hbm,
    b_head_hbm,
    latents,
    pick,
    raw,
    patches,
    wide_in,
    wide_down,
    wide_head,
    gain_in,
    gain_down,
    bias_down,
    partial,
    merged,
    frames,
    len_row,
    reader_row,
    owner_row,
    spread,
    w_in,
    b_in,
    g_in,
    w_down,
    b_down,
    g_down,
    w_head,
    b_head,
    len_s,
    reader_s,
    arrived,
):
    fetches = {}
    for n, (source, target) in enumerate(
        (
            (frames_hbm, frames),
            (len_row_hbm, len_row),
            (reader_row_hbm, reader_row),
            (owner_row_hbm, owner_row),
            (spread_hbm, spread),
            (w_in_hbm, w_in),
            (b_in_hbm, b_in),
            (g_in_hbm, g_in),
            (w_down_hbm, w_down),
            (b_down_hbm, b_down),
            (g_down_hbm, g_down),
            (w_head_hbm, w_head),
            (b_head_hbm, b_head),
            (len_row_hbm, len_s),
            (reader_row_hbm, reader_s),
        )
    ):
        fetches[n] = pltpu.make_async_copy(source, target, arrived.at[n])
        fetches[n].start()
    me = lax.axis_index("wide")
    read_rows = frames.shape[0]
    clips = len_s.shape[1]
    rows = latents.shape[0]

    order = arrangement(
        512,
        lambda i: ((i & 32) << 3) | ((i & 1) << 7) | ((i & 448) >> 2) | ((i & 30) >> 1),
    )
    for n in (0, 13, 14):
        fetches[n].wait()

    len0 = jnp.int32(0)
    len1 = jnp.int32(0)
    for c in range(clips):
        mine = reader_s[0, c] == me
        length = len_s[0, c]
        len1 = jnp.where(mine & (len0 > 0), length, len1)
        len0 = jnp.where(mine & (len0 == 0), length, len0)
    frames0 = 4 * len0 - 3

    split = []
    for h in range(2):
        piece = jnp.concatenate(
            [frames[:, k * 1024 + h * 512 : k * 1024 + (h + 1) * 512] for k in range(3)], axis=0
        )
        split.append(dot(piece, order))
    lane = iota((read_rows, 128), 1)
    across = lane & 15
    inside = {-1: across > 0, 1: across < 15}
    split = [part.astype(BF16) for part in split]
    zero = jnp.zeros((), BF16)
    for k in range(3):
        for r in range(4):
            for s in range(4):
                p = ((r + 1) % 2) * 2 + (s + 1) % 2
                low, high = (
                    part[k * read_rows : (k + 1) * read_rows, p * 128 : (p + 1) * 128]
                    for part in split
                )
                dy, dx = (-1, 0, 0, 1)[r], (-1, 0, 0, 1)[s]
                shift = -(dy * 16 + dx) % 128
                if shift:
                    low, high = pltpu.roll(low, shift, 1), pltpu.roll(high, shift, 1)
                if dy < 0:
                    low, high = jnp.where(lane < 16, zero, low), jnp.where(lane < 16, low, high)
                if dy > 0:
                    low, high = jnp.where(lane < 112, low, high), jnp.where(lane < 112, high, zero)
                if dx:
                    low, high = jnp.where(inside[dx], low, zero), jnp.where(inside[dx], high, zero)
                at = (k * 16 + r * 4 + s) * (read_rows + 1)
                raw[0, at : at + read_rows, :] = low.astype(F32)
                raw[1, at : at + read_rows, :] = high.astype(F32)

    def place(frame, carry):
        slot = frame + 2 + jnp.where(frame >= frames0, 2, 0)
        to = pl.multiple_of(slot * TAP, TAP)
        for h in range(2):
            patches[h, pl.ds(to, TAP), :] = raw[
                h, pl.ds(frame, TAP, stride=read_rows + 1), :
            ].astype(BF16)
        return carry

    for frame in range(read_rows):
        place(frame, 0)
    for n in range(1, 13):
        fetches[n].wait()

    pick[...] = pick_rows(
        me, steps, rows, pick.shape[0], len_row[...], reader_row[...], owner_row[...]
    )

    gain_in[...] = jnp.broadcast_to(column(g_in[...]) * 0.5, gain_in.shape)
    gain_down[...] = jnp.broadcast_to(column(g_down[...]) * 0.5, gain_down.shape)
    bias_down[...] = jnp.broadcast_to(column(b_down[...]), bias_down.shape)
    bias = column(b_in[...])
    bias_high = bias.astype(BF16).astype(F32)
    bias_mid = (bias - bias_high).astype(BF16).astype(F32)
    bias_low = bias - bias_high - bias_mid
    lane = iota((128, DEPTH), 1)
    bias_lanes = jnp.where(
        lane == 144,
        bias_high,
        jnp.where(lane == 145, bias_mid, jnp.where(lane == 146, bias_low, 0.0)),
    )
    for p in range(4):
        taps = lax.dot_general(
            w_in[...], spread[p], (((0,), (0,)), ((), ())), preferred_element_type=F32
        )
        wide_in[p * 128 : (p + 1) * 128, :] = (taps + bias_lanes).astype(BF16)
    order = arrangement(512, lambda i: ((i & 3) << 7) | (i >> 2))
    wide_down[...] = dot(w_down[...], order).astype(BF16)
    order = arrangement(256, lambda i: ((i & 15) << 4) | (i >> 4))
    chunks = []
    for chunk in range(8):
        piece = jnp.concatenate(
            [w_head[:, s * 2048 + chunk * 256 : s * 2048 + (chunk + 1) * 256] for s in range(4)],
            axis=0,
        )
        chunks.append(dot(piece, order).astype(BF16))
    group = iota((64, 128), 1) >> 4
    for half in range(2):
        parts = [chunk[:, half * 128 : (half + 1) * 128] for chunk in chunks]
        for bit in (1, 2, 4):
            upper = (group & bit) != 0
            for i in range(8):
                if i & bit:
                    continue
                low, high = parts[i], parts[i | bit]
                parts[i] = jnp.where(upper, pltpu.roll(high, bit * 16, 1), low)
                parts[i | bit] = jnp.where(upper, high, pltpu.roll(low, 128 - bit * 16, 1))
        for i in range(8):
            at = (half * 8 + i) * 16
            for s in range(4):
                wide_head[at : at + 16, s * 128 : (s + 1) * 128] = parts[i][
                    s * 16 : (s + 1) * 16
                ]

    patches[:, : 2 * TAP, :] = jnp.zeros((2, 2 * TAP, 128), BF16)
    patches[:, pl.ds(pl.multiple_of((frames0 + 2) * TAP, TAP), 2 * TAP), :] = jnp.zeros(
        (2, 2 * TAP, 128), BF16
    )

    square = iota((1, 256), 1)
    corner = ((square >> 4 & 3) << 2) | (square & 3)
    ones = jnp.ones((16, 256), BF16)

    def columns_of(frame):
        at = pl.ds(pl.multiple_of(frame * TAP, TAP), 3 * TAP)
        taps = jnp.concatenate([patches[0, at, :], patches[1, at, :]], axis=1)
        return jnp.concatenate([taps, ones], axis=0)

    def convolve(columns):
        product = dot(wide_in[...], columns)
        return jnp.concatenate(
            [
                half_silu_norm(product[p * 128 : (p + 1) * 128], twice(gain_in[...]), False)
                for p in range(4)
            ],
            axis=0,
        )

    def lower(columns):
        return half_silu_norm(
            dot(wide_down[...], columns) + twice(bias_down[...]), twice(gain_down[...]), False
        )

    def keep(row, product):
        total = jnp.zeros((16, 256), F32)
        for ab in range(16):
            total = total + jnp.where(corner == ab, product[ab * 16 : (ab + 1) * 16], 0.0)
        partial[pl.ds(pl.multiple_of(row * 16, 16), 16), :] = total

    partial[...] = jnp.zeros_like(partial)

    def opening(base):
        columns = columns_of(base)
        return dot(wide_head[:, 384:], lower(convolve(columns)))

    count = len0 + len1 - 2

    def first_frame(i):
        second = i >= len0 - 1
        j = i + 1 - jnp.where(second, len0 - 1, 0)
        return 4 * j - 3 + jnp.where(second, frames0 + 2, 0)

    def first_half(i):
        first = first_frame(i)
        for s in range(4):
            full = convolve(columns_of(first + s))
            merged[s, 0], merged[s, 1] = full[:, :128], full[:, 128:]

    def held(s):
        return jnp.concatenate([merged[s, 0], merged[s, 1]], axis=1)

    def hold(s, full):
        merged[s, 0], merged[s, 1] = full[:, :128], full[:, 128:]

    def row_of(i):
        return jnp.where(count > 0, i + 1 + jnp.where(i >= len0 - 1, 1, 0), rows)

    def head(i, reduced):
        keep(row_of(i), dot(wide_head[...], jnp.concatenate(reduced, axis=0)))

    keep(0, opening(0))
    first_half(0)

    def turns(i, n):
        full = [held(s) for s in range(4)]
        for d in range(n):
            first = first_frame(i + d + 1)
            reduced, behind = [], []
            for s in range(4):
                reduced.append(lower(full[s]))
                behind.append(convolve(columns_of(first + s)))
                if d == n - 1:
                    hold(s, behind[s])
            head(i + d, reduced)
            full = behind

    blocks = jnp.maximum(count - 1, 0) // BLOCK

    def block(k, carry):
        turns(BLOCK * k, BLOCK)
        return carry

    def single(i, carry):
        turns(i, 1)
        return carry

    lax.fori_loop(0, blocks, block, 0)
    lax.fori_loop(BLOCK * blocks, count - 1, single, 0)
    head(count - 1, [lower(held(s)) for s in range(4)])
    keep(len0, opening(frames0 + 2))

    place_of = iota((256, 128), 0)
    cell = ((place_of >> 6) << 2) | ((place_of & 15) >> 2)
    sums = one_hot(cell == (iota((256, 128), 1) & 15))
    sums = jnp.concatenate([sums, sums], axis=1)
    sums_of = partial[: rows * 16, :]
    high = sums_of.astype(BF16)
    spots = dot(high, sums) + dot((sums_of - high.astype(F32)).astype(BF16), sums)
    channel = (iota((16, 256), 1) >> 4) == iota((16, 256), 0)
    bias = jnp.sum(jnp.where(channel, column(b_head[...]), 0.0), axis=0, keepdims=True)
    spots = jnp.where(channel[None], spots.reshape(rows, 16, 256), 0.0)
    latents[...] = (jnp.sum(spots, axis=1) + bias).astype(BF16)


def encode(steps, own_rows, rows, frames, latent_len, reader, owner, weights):
    w_in, b_in, g_in, w_down, b_down, g_down, w_head, b_head = weights
    read_rows = frames.shape[0]
    vmem = pl.BlockSpec(memory_space=pltpu.VMEM)
    row = lambda x: x.reshape(1, -1)
    arrays = [
        frames,
        row(latent_len),
        row(reader),
        row(owner),
        patch_spread(),
        w_in.T,
        row(b_in),
        row(g_in),
        w_down,
        row(b_down),
        row(g_down),
        w_head,
        row(b_head),
    ]
    return pl.pallas_call(
        functools.partial(encode_kernel, steps),
        out_shape=(
            pltpu.VMEM((rows, 256), BF16),
            pltpu.VMEM((own_rows, rows << len(steps)), BF16),
        ),
        in_specs=[pl.BlockSpec(memory_space=pl.ANY)] * 13,
        out_specs=(vmem, vmem),
        scratch_shapes=[
            pltpu.VMEM((2, (read_rows + 1) * TAP, 128), F32),
            pltpu.VMEM((2, (read_rows + 4) * TAP, 128), BF16),
            pltpu.VMEM((512, DEPTH), BF16),
            pltpu.VMEM((128, 512), BF16),
            pltpu.VMEM((256, 512), BF16),
            pltpu.VMEM((128, 128), F32),
            pltpu.VMEM((128, 128), F32),
            pltpu.VMEM((128, 128), F32),
            pltpu.VMEM((rows * 16 + 16, 256), F32),
            pltpu.VMEM((4, 2, 512, 128), BF16),
        ]
        + [pltpu.VMEM(x.shape, x.dtype) for x in arrays]
        + [pltpu.SMEM((1, latent_len.shape[0]), jnp.int32)] * 2
        + [
            pltpu.SemaphoreType.DMA((15,)),
        ],
    )(*arrays)


def shards(
    frames, latent_len, reader, owner, w_in, b_in, g_in, w_down, b_down, g_down, w_head, b_head
):
    weights = (w_in, b_in, g_in, w_down, b_down, g_down, w_head, b_head)
    wide_n = lax.axis_size("wide")
    steps = []
    step = wide_n // 2
    while step > 1:
        steps.append(step + 1)
        step //= 2
    steps.append(1)
    most_read = frames.shape[0] // 4
    own_rows = 2 * ((most_read + 2) // 2)
    rows = -(-most_read // 16) * 16
    latents, pick = encode(steps, own_rows, rows, frames, latent_len, reader, owner, weights)
    for step in steps:
        pairs = [(i, i ^ step) for i in range(wide_n)]
        latents = jnp.concatenate([latents, lax.ppermute(latents, "wide", pairs)], axis=0)
    return jnp.dot(pick, latents, preferred_element_type=F32).astype(BF16)


def solution(mesh):
    return jax.shard_map(
        shards,
        mesh=mesh,
        in_specs=(P(("groups", "wide"), None), P("groups"), P("groups"), P("groups")) + (P(),) * 8,
        out_specs=P(("groups", "wide"), None),
        check_vma=False,
    )
```

```python
import functools

import jax
import jax.numpy as jnp
import numpy as np
from jax import lax
from jax.experimental import pallas as pl
from jax.experimental.pallas import tpu as pltpu
from jax.sharding import PartitionSpec as P

PIX = 32
EPS = 1e-06
TAP = 48
DEPTH = 160
F32 = jnp.float32
BF16 = jnp.bfloat16


def patch_spread():
    spread = np.zeros((4, 81, DEPTH), np.float32)
    for a2 in range(2):
        for b2 in range(2):
            for t in range(3):
                for a in range(3):
                    for b in range(3):
                        for k in range(3):
                            row = t * 27 + (a * 3 + b) * 3 + k
                            col = t * TAP + k * 16 + (a2 + a) * 4 + b2 + b
                            spread[2 * a2 + b2, row, col] = 1
    return jnp.asarray(spread, BF16)


def iota(shape, axis):
    return lax.broadcasted_iota(jnp.int32, shape, axis)


def one_hot(flags):
    return jnp.where(flags, 1.0, 0.0).astype(BF16)


def dot(a, b):
    return jnp.dot(a, b, preferred_element_type=F32)


def twice(x):
    return jnp.concatenate([x, x], axis=1)


def arrangement(size, move):
    to = move(iota((size, 128), 0))
    lane = iota((size, 128), 1)
    return jnp.concatenate([one_hot(to == lane + at) for at in range(0, size, 128)], axis=1)


def column(row):
    n = row.shape[1]
    eye = iota((n, n), 0) == iota((n, n), 1)
    return jnp.sum(jnp.where(eye, row, 0.0), axis=1, keepdims=True)


def half_silu_norm(values, half_gain, narrow):
    mean_square = jnp.sum(values * values, axis=0, keepdims=True) * (1.0 / values.shape[0])
    h = values * lax.rsqrt(mean_square + EPS) * half_gain
    if narrow:
        h = h.astype(BF16)
    return (h + h * jnp.tanh(h)).astype(BF16)


def pick_rows(me, steps, rows, own_rows, len_row, reader_row, owner_row):
    clips = len_row.shape[1]
    lens = len_row.astype(F32)
    len_col = column(lens)
    reader_col = column(reader_row.astype(F32))
    owner_col = column(owner_row.astype(F32))
    earlier = iota((clips, clips), 0) < iota((clips, clips), 1)
    same_reader = reader_col == reader_row.astype(F32)
    same_owner = owner_col == owner_row.astype(F32)
    read_off = jnp.sum(jnp.where(earlier & same_reader, len_col, 0.0), axis=0, keepdims=True)
    own_off = jnp.sum(jnp.where(earlier & same_owner, len_col, 0.0), axis=0, keepdims=True)
    away = reader_row ^ me
    block = jnp.zeros_like(away)
    core = away & 1
    for at, step in enumerate(steps[:-1]):
        across = jnp.where((away & (step - 1)) != 0, 1, 0)
        core = core ^ across
        block = block | (across << at)
    block = block | (core << (len(steps) - 1))
    slot = iota((own_rows, clips), 0).astype(F32)
    inside = (owner_row == me) & (own_off <= slot) & (slot < own_off + lens)
    source = block.astype(F32) * rows + read_off - own_off + slot
    source = jnp.sum(jnp.where(inside, source + 1.0, 0.0), axis=1, keepdims=True) - 1.0
    width = rows << len(steps)
    return one_hot(iota((own_rows, width), 1).astype(F32) == source)


BLOCKS = (12, 4, 1)


def encode_kernel(
    steps,
    frames_hbm,
    len_row_hbm,
    reader_row_hbm,
    owner_row_hbm,
    spread_hbm,
    w_in_hbm,
    b_in_hbm,
    g_in_hbm,
    w_down_hbm,
    b_down_hbm,
    g_down_hbm,
    w_head_hbm,
    b_head_hbm,
    latents,
    pick,
    raw,
    patches,
    wide_in,
    wide_down,
    wide_head,
    gain_in,
    gain_down,
    bias_down,
    partial,
    merged,
    frames,
    len_row,
    reader_row,
    owner_row,
    spread,
    w_in,
    b_in,
    g_in,
    w_down,
    b_down,
    g_down,
    w_head,
    b_head,
    len_s,
    reader_s,
    arrived,
):
    fetches = {}
    for n, (source, target) in enumerate(
        (
            (frames_hbm, frames),
            (len_row_hbm, len_row),
            (reader_row_hbm, reader_row),
            (owner_row_hbm, owner_row),
            (spread_hbm, spread),
            (w_in_hbm, w_in),
            (b_in_hbm, b_in),
            (g_in_hbm, g_in),
            (w_down_hbm, w_down),
            (b_down_hbm, b_down),
            (g_down_hbm, g_down),
            (w_head_hbm, w_head),
            (b_head_hbm, b_head),
            (len_row_hbm, len_s),
            (reader_row_hbm, reader_s),
        )
    ):
        fetches[n] = pltpu.make_async_copy(source, target, arrived.at[n])
        fetches[n].start()
    me = lax.axis_index("wide")
    read_rows = frames.shape[0]
    clips = len_s.shape[1]
    rows = latents.shape[0]

    order = arrangement(
        512,
        lambda i: ((i & 32) << 3) | ((i & 1) << 7) | ((i & 448) >> 2) | ((i & 30) >> 1),
    )
    for n in (0, 13, 14):
        fetches[n].wait()

    len0 = jnp.int32(0)
    len1 = jnp.int32(0)
    for c in range(clips):
        mine = reader_s[0, c] == me
        length = len_s[0, c]
        len1 = jnp.where(mine & (len0 > 0), length, len1)
        len0 = jnp.where(mine & (len0 == 0), length, len0)
    frames0 = 4 * len0 - 3

    split = []
    for h in range(2):
        piece = jnp.concatenate(
            [frames[:, k * 1024 + h * 512 : k * 1024 + (h + 1) * 512] for k in range(3)], axis=0
        )
        split.append(dot(piece, order))
    lane = iota((read_rows, 128), 1)
    across = lane & 15
    inside = {-1: across > 0, 1: across < 15}
    split = [part.astype(BF16) for part in split]
    zero = jnp.zeros((), BF16)
    for k in range(3):
        for r in range(4):
            for s in range(4):
                p = ((r + 1) % 2) * 2 + (s + 1) % 2
                low, high = (
                    part[k * read_rows : (k + 1) * read_rows, p * 128 : (p + 1) * 128]
                    for part in split
                )
                dy, dx = (-1, 0, 0, 1)[r], (-1, 0, 0, 1)[s]
                shift = -(dy * 16 + dx) % 128
                if shift:
                    low, high = pltpu.roll(low, shift, 1), pltpu.roll(high, shift, 1)
                if dy < 0:
                    low, high = jnp.where(lane < 16, zero, low), jnp.where(lane < 16, low, high)
                if dy > 0:
                    low, high = jnp.where(lane < 112, low, high), jnp.where(lane < 112, high, zero)
                if dx:
                    low, high = jnp.where(inside[dx], low, zero), jnp.where(inside[dx], high, zero)
                at = (k * 16 + r * 4 + s) * (read_rows + 1)
                raw[0, at : at + read_rows, :] = low.astype(F32)
                raw[1, at : at + read_rows, :] = high.astype(F32)

    def place(frame, carry):
        slot = frame + 2 + jnp.where(frame >= frames0, 2, 0)
        to = pl.multiple_of(slot * TAP, TAP)
        for h in range(2):
            patches[h, pl.ds(to, TAP), :] = raw[
                h, pl.ds(frame, TAP, stride=read_rows + 1), :
            ].astype(BF16)
        return carry

    for frame in range(read_rows):
        place(frame, 0)
    for n in range(1, 13):
        fetches[n].wait()

    pick[...] = pick_rows(
        me, steps, rows, pick.shape[0], len_row[...], reader_row[...], owner_row[...]
    )

    gain_in[...] = jnp.broadcast_to(column(g_in[...]) * 0.5, gain_in.shape)
    gain_down[...] = jnp.broadcast_to(column(g_down[...]) * 0.5, gain_down.shape)
    bias_down[...] = jnp.broadcast_to(column(b_down[...]), bias_down.shape)
    bias = column(b_in[...])
    bias_high = bias.astype(BF16).astype(F32)
    bias_mid = (bias - bias_high).astype(BF16).astype(F32)
    bias_low = bias - bias_high - bias_mid
    lane = iota((128, DEPTH), 1)
    bias_lanes = jnp.where(
        lane == 144,
        bias_high,
        jnp.where(lane == 145, bias_mid, jnp.where(lane == 146, bias_low, 0.0)),
    )
    for p in range(4):
        taps = lax.dot_general(
            w_in[...], spread[p], (((0,), (0,)), ((), ())), preferred_element_type=F32
        )
        wide_in[p * 128 : (p + 1) * 128, :] = (taps + bias_lanes).astype(BF16)
    order = arrangement(512, lambda i: ((i & 3) << 7) | (i >> 2))
    wide_down[...] = dot(w_down[...], order).astype(BF16)
    order = arrangement(256, lambda i: ((i & 15) << 4) | (i >> 4))
    chunks = []
    for chunk in range(8):
        piece = jnp.concatenate(
            [w_head[:, s * 2048 + chunk * 256 : s * 2048 + (chunk + 1) * 256] for s in range(4)],
            axis=0,
        )
        chunks.append(dot(piece, order).astype(BF16))
    group = iota((64, 128), 1) >> 4
    for half in range(2):
        parts = [chunk[:, half * 128 : (half + 1) * 128] for chunk in chunks]
        for bit in (1, 2, 4):
            upper = (group & bit) != 0
            for i in range(8):
                if i & bit:
                    continue
                low, high = parts[i], parts[i | bit]
                parts[i] = jnp.where(upper, pltpu.roll(high, bit * 16, 1), low)
                parts[i | bit] = jnp.where(upper, high, pltpu.roll(low, 128 - bit * 16, 1))
        for i in range(8):
            at = (half * 8 + i) * 16
            for s in range(4):
                wide_head[at : at + 16, s * 128 : (s + 1) * 128] = parts[i][
                    s * 16 : (s + 1) * 16
                ]

    patches[:, : 2 * TAP, :] = jnp.zeros((2, 2 * TAP, 128), BF16)
    patches[:, pl.ds(pl.multiple_of((frames0 + 2) * TAP, TAP), 2 * TAP), :] = jnp.zeros(
        (2, 2 * TAP, 128), BF16
    )

    square = iota((1, 256), 1)
    corner = ((square >> 4 & 3) << 2) | (square & 3)
    ones = jnp.ones((16, 256), BF16)

    def columns_of(frame):
        at = pl.ds(pl.multiple_of(frame * TAP, TAP), 3 * TAP)
        taps = jnp.concatenate([patches[0, at, :], patches[1, at, :]], axis=1)
        return jnp.concatenate([taps, ones], axis=0)

    def convolve(columns):
        product = dot(wide_in[...], columns)
        return jnp.concatenate(
            [
                half_silu_norm(product[p * 128 : (p + 1) * 128], twice(gain_in[...]), False)
                for p in range(4)
            ],
            axis=0,
        )

    def lower(columns):
        return half_silu_norm(
            dot(wide_down[...], columns) + twice(bias_down[...]), twice(gain_down[...]), False
        )

    def keep(row, product):
        total = jnp.zeros((16, 256), F32)
        for ab in range(16):
            total = total + jnp.where(corner == ab, product[ab * 16 : (ab + 1) * 16], 0.0)
        partial[pl.ds(pl.multiple_of(row * 16, 16), 16), :] = total

    partial[...] = jnp.zeros_like(partial)

    def opening(base):
        columns = columns_of(base)
        return dot(wide_head[:, 384:], lower(convolve(columns)))

    count = len0 + len1 - 2

    def first_frame(i):
        second = i >= len0 - 1
        j = i + 1 - jnp.where(second, len0 - 1, 0)
        return 4 * j - 3 + jnp.where(second, frames0 + 2, 0)

    def first_half(i):
        first = first_frame(i)
        for s in range(4):
            full = convolve(columns_of(first + s))
            merged[s, 0], merged[s, 1] = full[:, :128], full[:, 128:]

    def held(s):
        return jnp.concatenate([merged[s, 0], merged[s, 1]], axis=1)

    def hold(s, full):
        merged[s, 0], merged[s, 1] = full[:, :128], full[:, 128:]

    def row_of(i):
        return jnp.where(count > 0, i + 1 + jnp.where(i >= len0 - 1, 1, 0), rows)

    def head(i, reduced):
        keep(row_of(i), dot(wide_head[...], jnp.concatenate(reduced, axis=0)))

    keep(0, opening(0))
    first_half(0)

    def turns(i, n):
        full = [held(s) for s in range(4)]
        for d in range(n):
            first = first_frame(i + d + 1)
            reduced, behind = [], []
            for s in range(4):
                reduced.append(lower(full[s]))
                behind.append(convolve(columns_of(first + s)))
                if d == n - 1:
                    hold(s, behind[s])
            head(i + d, reduced)
            full = behind

    done = jnp.int32(0)
    for n in BLOCKS:
        trips = jnp.maximum(count - 1 - done, 0) // n

        def block(k, carry, n=n, done=done):
            turns(done + n * k, n)
            return carry

        lax.fori_loop(0, trips, block, 0)
        done = done + n * trips

    head(count - 1, [lower(held(s)) for s in range(4)])
    keep(len0, opening(frames0 + 2))

    place_of = iota((256, 128), 0)
    cell = ((place_of >> 6) << 2) | ((place_of & 15) >> 2)
    sums = one_hot(cell == (iota((256, 128), 1) & 15))
    sums = jnp.concatenate([sums, sums], axis=1)
    sums_of = partial[: rows * 16, :]
    high = sums_of.astype(BF16)
    spots = dot(high, sums) + dot((sums_of - high.astype(F32)).astype(BF16), sums)
    channel = (iota((16, 256), 1) >> 4) == iota((16, 256), 0)
    bias = jnp.sum(jnp.where(channel, column(b_head[...]), 0.0), axis=0, keepdims=True)
    spots = jnp.where(channel[None], spots.reshape(rows, 16, 256), 0.0)
    latents[...] = (jnp.sum(spots, axis=1) + bias).astype(BF16)


def encode(steps, own_rows, rows, frames, latent_len, reader, owner, weights):
    w_in, b_in, g_in, w_down, b_down, g_down, w_head, b_head = weights
    read_rows = frames.shape[0]
    vmem = pl.BlockSpec(memory_space=pltpu.VMEM)
    row = lambda x: x.reshape(1, -1)
    arrays = [
        frames,
        row(latent_len),
        row(reader),
        row(owner),
        patch_spread(),
        w_in.T,
        row(b_in),
        row(g_in),
        w_down,
        row(b_down),
        row(g_down),
        w_head,
        row(b_head),
    ]
    return pl.pallas_call(
        functools.partial(encode_kernel, steps),
        out_shape=(
            pltpu.VMEM((rows, 256), BF16),
            pltpu.VMEM((own_rows, rows << len(steps)), BF16),
        ),
        in_specs=[pl.BlockSpec(memory_space=pl.ANY)] * 13,
        out_specs=(vmem, vmem),
        scratch_shapes=[
            pltpu.VMEM((2, (read_rows + 1) * TAP, 128), F32),
            pltpu.VMEM((2, (read_rows + 4) * TAP, 128), BF16),
            pltpu.VMEM((512, DEPTH), BF16),
            pltpu.VMEM((128, 512), BF16),
            pltpu.VMEM((256, 512), BF16),
            pltpu.VMEM((128, 128), F32),
            pltpu.VMEM((128, 128), F32),
            pltpu.VMEM((128, 128), F32),
            pltpu.VMEM((rows * 16 + 16, 256), F32),
            pltpu.VMEM((4, 2, 512, 128), BF16),
        ]
        + [pltpu.VMEM(x.shape, x.dtype) for x in arrays]
        + [pltpu.SMEM((1, latent_len.shape[0]), jnp.int32)] * 2
        + [
            pltpu.SemaphoreType.DMA((15,)),
        ],
    )(*arrays)


def shards(
    frames, latent_len, reader, owner, w_in, b_in, g_in, w_down, b_down, g_down, w_head, b_head
):
    weights = (w_in, b_in, g_in, w_down, b_down, g_down, w_head, b_head)
    wide_n = lax.axis_size("wide")
    steps = []
    step = wide_n // 2
    while step > 1:
        steps.append(step + 1)
        step //= 2
    steps.append(1)
    most_read = frames.shape[0] // 4
    own_rows = 2 * ((most_read + 2) // 2)
    rows = -(-most_read // 16) * 16
    latents, pick = encode(steps, own_rows, rows, frames, latent_len, reader, owner, weights)
    for step in steps:
        pairs = [(i, i ^ step) for i in range(wide_n)]
        latents = jnp.concatenate([latents, lax.ppermute(latents, "wide", pairs)], axis=0)
    return jnp.dot(pick, latents, preferred_element_type=F32).astype(BF16)


def solution(mesh):
    return jax.shard_map(
        shards,
        mesh=mesh,
        in_specs=(P(("groups", "wide"), None), P("groups"), P("groups"), P("groups")) + (P(),) * 8,
        out_specs=P(("groups", "wide"), None),
        check_vma=False,
    )
```
